256 devices in a mesh: ctx: 32 (over z, y_hi, core), head: 8 (over y_lo, x).
Axes of the slice: x: 4, y: 4 (y_hi: 2, y_lo: 2; y = y_hi * 2 + y_lo), z: 8, core: 2. Of those that a mesh axis runs over, the one named last changes fastest.
Arguments:
- query1: bfloat16 [16384, 6144], P('ctx', 'head'), may hold values from -6 to 6
- key1: bfloat16 [16384, 6144], P('ctx', 'head'), may hold values from -6 to 6
- value1: bfloat16 [16384, 6144], P('ctx', 'head'), may hold values from -50 to 50
- log_decay: float32 [16384, 64], P('ctx', 'head'), may hold values from -1 to 0
- out_weight: bfloat16 [6144, 3072], P('head'), may hold values from -0.078125 to 0.078125
- query2: bfloat16 [16384, 6144], P('ctx', 'head'), may hold values from -12 to 12
- key2: bfloat16 [16384, 6144], P('ctx', 'head'), may hold values from -6 to 6
- value2: bfloat16 [16384, 6144], P('ctx', 'head'), may hold values from -6 to 6
Outputs:
- linear_mixed: bfloat16 [16384, 3072], P(('ctx', 'head'))
- attended: bfloat16 [16384, 6144], P('ctx', 'head')
The draws below stay inside these ranges and needn't reach their ends.
All inputs are finite; a program needn't handle non-finite values.
Results may differ from the reference program's by a relative error of at most 0.017.
Values may be sent and summed in bfloat16 or wider, within the bound.
A program may use at most 64 MiB of HBM per device.

```python
import math
import jax
import jax.numpy as jnp
from jax import lax

HEAD_TOTAL = 64
DH = 96
LBLOCK = 256
PROJ = 3072
TOK_DEV = 512
TOKEN_TOTAL = 16384
WINDOW = 1536


def clipped_normal(key, shape, bound):
    return jnp.clip(jax.random.normal(key, shape, jnp.float32), -bound, bound)


def draw_query2(key, part):
    values = clipped_normal(jax.random.fold_in(key, 1), (TOKEN_TOTAL, HEAD_TOTAL * DH), 6.0)
    return values.astype(jnp.bfloat16)


def draw_key2(key, part):
    values = clipped_normal(jax.random.fold_in(key, 3), (TOKEN_TOTAL, HEAD_TOTAL * DH), 6.0)
    return values.astype(jnp.bfloat16)


def draw_value1(key, part):
    column_scale = jnp.exp(jax.random.uniform(jax.random.fold_in(key, 21), (1, HEAD_TOTAL * DH), jnp.float32, -1.15, 1.15))
    row_scale = jnp.exp(jax.random.uniform(jax.random.fold_in(key, 22), (TOKEN_TOTAL, 1), jnp.float32, -1.15, 1.15))
    values = clipped_normal(jax.random.fold_in(key, 25), (TOKEN_TOTAL, HEAD_TOTAL * DH), 5.0)
    return (values * column_scale * row_scale).astype(jnp.bfloat16)


def draw_log_decay(key, part):
    fast_share = 0.35
    fast = jax.random.uniform(jax.random.fold_in(key, 31), (HEAD_TOTAL,), jnp.float32) < fast_share
    fast_rate = math.log(10.0) * jax.random.uniform(jax.random.fold_in(key, 32), (HEAD_TOTAL,), jnp.float32, 1.0 / 50.0, 1.0 / 30.0)
    slow_log = jax.random.uniform(jax.random.fold_in(key, 33), (HEAD_TOTAL,), jnp.float32, math.log(1.0 / 32.0), math.log(1.0 / 8.0))
    slow_rate = math.log(10.0) / TOKEN_TOTAL * jnp.exp(slow_log)
    baseline_speed = jnp.where(fast, fast_rate, slow_rate)
    processor_multiplier = jnp.exp(jax.random.uniform(jax.random.fold_in(key, 34), (TOKEN_TOTAL // TOK_DEV, HEAD_TOTAL), jnp.float32, -0.7, 0.7))
    processor_multiplier = jnp.repeat(processor_multiplier, TOK_DEV, axis=0)
    token_multiplier = jax.random.uniform(jax.random.fold_in(key, 35), (TOKEN_TOTAL, HEAD_TOTAL), jnp.float32, 0.5, 1.5)
    spike_amount = jax.random.uniform(jax.random.fold_in(key, 36), (TOKEN_TOTAL, HEAD_TOTAL), jnp.float32) < 4.0 / TOKEN_TOTAL
    spike_penalty = jnp.log(jax.random.uniform(jax.random.fold_in(key, 37), (TOKEN_TOTAL, HEAD_TOTAL), jnp.float32, 0.5, 0.8))
    return -(baseline_speed[None, :] * processor_multiplier * token_multiplier) + jnp.where(spike_amount, spike_penalty, 0.0)


def block_levels(key, shape, cuts, smallest, top_value):
    factor_of = 1.0
    for dim, blocks in cuts:
        steps = jax.random.uniform(jax.random.fold_in(jax.random.fold_in(key, 6), dim), (blocks,), jnp.float32, smallest / len(cuts), top_value / len(cuts))
        factor_of = factor_of * jnp.repeat(jnp.exp(steps), shape[dim] // blocks).reshape((-1,) + (1,) * (len(shape) - 1 - dim))
    return factor_of


def normal_values(own_key, shape, spread, limit, split=(), held_as=jnp.bfloat16):
    array = jax.random.normal(own_key, shape, jnp.float32) * spread
    if len(split) > 0:
        array = block_levels(own_key, shape, split, -0.22, 0.18) * array
    return jnp.clip(array, min=-limit, max=limit).astype(held_as)


def setup_inputs(seed: int = 0) -> dict:
    keys = jax.random.split(jax.random.key(seed), 9)
    return {
        "query1": normal_values(keys[0], (TOKEN_TOTAL, HEAD_TOTAL * DH), 1.0, 6.0, ((0, 32), (1, 8))),
        "key1": normal_values(keys[1], (TOKEN_TOTAL, HEAD_TOTAL * DH), 1.0, 6.0, ((0, 32), (1, 8))),
        "value1": draw_value1(jax.random.fold_in(keys[8], 71), 0),
        "log_decay": draw_log_decay(jax.random.fold_in(keys[8], 71), 0),
        "out_weight": normal_values(keys[4], (HEAD_TOTAL * DH, PROJ), (HEAD_TOTAL * DH) ** -0.5, 0.078125, ((0, 8),)),
        "query2": draw_query2(jax.random.fold_in(keys[8], 71), 0),
        "key2": draw_key2(jax.random.fold_in(keys[8], 71), 0),
        "value2": normal_values(keys[7], (TOKEN_TOTAL, HEAD_TOTAL * DH), 1.0, 6.0, ((0, 32), (1, 8))),
    }


eps_norm = 1e-06

def block_scan(carry_state, pieces):
    query_part = pieces[0].astype(jnp.float32)
    key_part = pieces[1].astype(jnp.float32)
    value_part = pieces[2].astype(jnp.float32)
    decay_part = pieces[3]
    block_len = decay_part.shape[0]
    running = jnp.cumsum(decay_part, axis=0)
    by_head = running.T
    gaps_log = by_head[:, :, None] - by_head[:, None, :]
    causal = jnp.arange(block_len)[:, None] >= jnp.arange(block_len)[None, :]
    weight = jnp.exp(jnp.where(causal[None], gaps_log, -jnp.inf))
    scores = jnp.einsum('ihd,jhd->hij', query_part, key_part)
    mixing = (scores * weight).astype(jnp.bfloat16)
    mixing = lax.optimization_barrier(mixing).astype(jnp.float32)
    inside = jnp.einsum('hij,jhd->ihd', mixing, value_part)
    outside = jnp.einsum('ihd,hde->ihe', query_part * jnp.exp(running)[:, :, None], carry_state, precision=lax.Precision.HIGHEST)
    block_total = running[-1]
    update = jnp.einsum('jhd,jhe->hde', key_part * jnp.exp(block_total[None, :] - running)[:, :, None], value_part, precision=lax.Precision.HIGHEST)
    new_state = jnp.exp(block_total)[:, None, None] * carry_state + update
    return (new_state, inside + outside)

def reference(query1, key1, value1, log_decay, out_weight, query2, key2, value2):
    block_count = TOKEN_TOTAL // LBLOCK
    inputs = (query1.reshape(block_count, LBLOCK, HEAD_TOTAL, DH), key1.reshape(block_count, LBLOCK, HEAD_TOTAL, DH), value1.reshape(block_count, LBLOCK, HEAD_TOTAL, DH), log_decay.reshape(block_count, LBLOCK, HEAD_TOTAL))
    final_state, outputs = lax.scan(block_scan, jnp.zeros((HEAD_TOTAL, DH, DH), jnp.float32), inputs)
    combined = outputs.reshape(TOKEN_TOTAL, HEAD_TOTAL, DH)
    mean_square = lax.optimization_barrier(jnp.mean(combined * combined, axis=-1, keepdims=True))
    normed = (combined / jnp.sqrt(mean_square + eps_norm)).astype(jnp.bfloat16).reshape(TOKEN_TOTAL, HEAD_TOTAL * DH)
    linear_mixed = jnp.dot(normed, out_weight, preferred_element_type=jnp.float32).astype(jnp.bfloat16)
    query_rows = min(512, TOK_DEV)
    key_span = WINDOW + query_rows
    padded_keys = jnp.pad(key2, ((WINDOW, 0), (0, 0)))
    padded_values = jnp.pad(value2, ((WINDOW, 0), (0, 0)))
    score_scale = 1.0 / math.sqrt(DH)

    def attend_block(block_index):
        first_row = (block_index * query_rows).astype(jnp.int32)
        query_part = lax.dynamic_slice_in_dim(query2, first_row, query_rows, 0).reshape(query_rows, HEAD_TOTAL, DH)
        key_part = lax.dynamic_slice_in_dim(padded_keys, first_row, key_span, 0).reshape(key_span, HEAD_TOTAL, DH)
        value_part = lax.dynamic_slice_in_dim(padded_values, first_row, key_span, 0).reshape(key_span, HEAD_TOTAL, DH)
        scores = jnp.einsum('ihd,jhd->hij', query_part.astype(jnp.float32), key_part.astype(jnp.float32)) * score_scale
        query_pos = first_row + jnp.arange(query_rows, dtype=jnp.int32)[:, None]
        key_pos = first_row - WINDOW + jnp.arange(key_span, dtype=jnp.int32)[None, :]
        allowed = (key_pos <= query_pos) & (query_pos - key_pos < WINDOW) & (key_pos >= 0)
        scores = jnp.where(allowed[None], scores, -jnp.inf)
        row_peak = lax.optimization_barrier(jnp.max(scores, axis=-1, keepdims=True))
        exponent = jnp.exp(scores - row_peak)
        probability = (exponent / lax.optimization_barrier(jnp.sum(exponent, axis=-1, keepdims=True))).astype(jnp.bfloat16)
        result = jnp.einsum('hij,jhd->ihd', probability.astype(jnp.float32), value_part.astype(jnp.float32))
        return result.astype(jnp.bfloat16).reshape(query_rows, HEAD_TOTAL * DH)
    attended = lax.map(attend_block, jnp.arange(TOKEN_TOTAL // query_rows, dtype=jnp.int32)).reshape(TOKEN_TOTAL, HEAD_TOTAL * DH)
    return (linear_mixed, attended)
```

```python
import math

import jax
import jax.numpy as jnp
from jax import lax
from jax.experimental import pallas as pl
from jax.experimental.pallas import tpu as pltpu
from jax.sharding import PartitionSpec as P

DH = 96
ROWS = 512
COLS = 768
NH = 8
GW = 384
PROJ = 3072
HALF = PROJ // 2
WIN = 256
SPAN = 1792
NEG = -1e30
EPS = 1e-6
MESH = pl.DeviceIdType.MESH
F32 = jnp.float32
BF16 = jnp.bfloat16
HBM = pltpu.MemorySpace.HBM

HALO_FIRST = [(1, 0, 0)]
HALO_AFTER_A = [(0, 0, 0)]
HALO_AFTER_B = [(1, 1, 0)]
HALO_AFTER_C = [(0, 1, 0), (1, 0, 1), (0, 0, 1), (0, 1, 1), (1, 1, 1)]


def dot(a, b, ca, cb):
    return lax.dot_general(a, b, (((ca,), (cb,)), ((), ())), preferred_element_type=F32)


def lanes(shape):
    return lax.broadcasted_iota(jnp.int32, shape, len(shape) - 1)


def rows_of(shape):
    return lax.broadcasted_iota(jnp.int32, shape, len(shape) - 2)


def head_window(h):
    start = GW * lax.div(h, 4) + 128 * lax.div(lax.rem(h, 4), 2)
    return pl.multiple_of(start, 128), DH * h - start


def head_mask(low):
    lane = lanes((1, WIN))
    return (lane >= low) & (lane < low + DH)


def same_head(tile):
    row = lax.div(rows_of((GW, 128)), DH)
    col = lax.div(lanes((GW, 128)) + 128 * tile, DH)
    return row == col


def kernel(
    q1h, k1h, v1h, dec, wh, q2h, k2h, v2h,
    lin_out, att_out,
    q1, k1, v1, q2, kk, vv, w,
    dpad, crow, ct, cexp, acc, fold, dtot,
    recv_a, dec_a, tot_b, dec_s, recv_b, dec_b, pacc, send_c, recv_c,
    normed, part, x1s, x1r, x2s, x2r, ys, yr,
    s_scr, p_scr,
    load_sem, halo_send, halo_recv, fwd_send, a_send, a_recv, b_send, b_recv, c_send, c_recv,
    x_send, x_recv, y_send, y_recv,
):
    t, hd = lax.axis_index("ctx"), lax.axis_index("head")
    z, j, core = lax.div(t, 4), lax.rem(t, 4), lax.rem(t, 2)
    yl, x = lax.div(hd, 4), lax.rem(hd, 4)
    sibling = t + 1 - 2 * core
    x_up, x_down = yl * 4 + lax.rem(x + 1, 4), yl * 4 + lax.rem(x + 3, 4)
    y_other = (1 - yl) * 4 + x

    related = [
        (lax.rem(t + 2, 32), hd),
        (lax.rem(t + 30, 32), hd),
        (sibling, hd),
        (lax.rem(t + 29 + 6 * core, 32), hd),
        (t, x_up),
        (t, x_down),
        (t, y_other),
    ]
    related += [(4 * z + lax.rem(j + d, 4), hd) for d in (1, 2, 3)]
    related += [(lax.rem(t + 4 * d, 32), hd) for d in range(1, 8)]
    barrier = pltpu.get_barrier_semaphore()
    for device in related:
        pl.semaphore_signal(barrier, inc=1, device_id=device, device_id_type=MESH)

    own = pl.ds(3 * ROWS, ROWS)
    loads = [
        pltpu.make_async_copy(src, dst, load_sem.at[i])
        for i, (src, dst) in enumerate(
            [(k1h, k1), (v1h, v1), (q1h, q1), (q2h, q2), (k2h, kk.at[own]), (v2h, vv.at[own]), (wh, w)]
        )
    ]
    for copy in loads:
        copy.start()
    pl.semaphore_wait(barrier, len(related))

    def half(g):
        return pl.ds(GW * g, GW)

    def halo(kind, kv, g):
        src, dst = ((k2h, kk), (v2h, vv))[kv]
        slot = 1 if kind == 0 else 2 - 2 * core
        target = lax.rem(t + 2, 32) if kind == 0 else lax.rem(t + 1 + 2 * core, 32)
        return pltpu.make_async_remote_copy(
            src_ref=src.at[:, half(g)],
            dst_ref=dst.at[pl.ds(slot * ROWS, ROWS), half(g)],
            send_sem=halo_send.at[kind, kv, g],
            recv_sem=halo_recv.at[slot, kv, g],
            device_id=(target, hd),
            device_id_type=MESH,
        )

    def arrived(slot, kv, g):
        dst = (kk, vv)[kv].at[pl.ds(slot * ROWS, ROWS), half(g)]
        return pltpu.make_async_remote_copy(
            src_ref=dst,
            dst_ref=dst,
            send_sem=halo_send.at[0, kv, g],
            recv_sem=halo_recv.at[slot, kv, g],
            device_id=(sibling, hd),
            device_id_type=MESH,
        )

    def forward(kv, g):
        buf = (kk, vv)[kv]
        slot = 2 * core
        return pltpu.make_async_remote_copy(
            src_ref=buf.at[pl.ds(ROWS, ROWS), half(g)],
            dst_ref=buf.at[pl.ds(slot * ROWS, ROWS), half(g)],
            send_sem=fwd_send.at[kv, g],
            recv_sem=halo_recv.at[slot, kv, g],
            device_id=(sibling, hd),
            device_id_type=MESH,
        )

    for item in HALO_FIRST:
        halo(*item).start()

    dpad[...] = jnp.zeros_like(dpad)
    dpad[:, :NH] = dec[...]
    lower = (rows_of((ROWS, ROWS)) >= lanes((ROWS, ROWS))).astype(F32)
    running = lax.dot_general(
        lower, dpad[...], (((1,), (0,)), ((), ())), precision=lax.Precision.HIGHEST, preferred_element_type=F32
    )
    ct[...] = jnp.transpose(running)[:NH, :]
    for h in range(NH):
        crow[h] = jnp.broadcast_to(running[:, h : h + 1], (ROWS, 128))
    for h in range(NH):
        dtot[h : h + 1, :] = crow[h, ROWS - 1 : ROWS, :]
    lane = lanes((ROWS, 128))
    for g in range(2):
        for tile, cut in enumerate((96, 64, 32)):
            h = 4 * g + tile
            at = pl.ds(GW * g + 128 * tile, 128)
            cexp[:, at] = jnp.where(lane < cut, crow[h], crow[h + 1])

    loads[0].wait()
    loads[1].wait()
    for g in range(2):
        c = cexp[:, half(g)]
        kw = (k1[:, half(g)].astype(F32) * jnp.exp(cexp[ROWS - 1 : ROWS, half(g)] - c)).astype(BF16)
        full = dot(kw, v1[:, half(g)], 0, 0)
        total = jnp.zeros((GW, 128), F32)
        for tile in range(3):
            total += jnp.where(same_head(tile), full[:, 128 * tile : 128 * tile + 128], 0.0)
        fold[pl.ds(GW * g, GW), :] = total.astype(BF16)

    def two_heads(index):
        return pl.ds(pl.multiple_of(192 * index, 16), 192)

    a_copies = []
    for d in (1, 2, 3):
        to = lax.rem(j + d, 4)
        for n, (src, dst) in enumerate([(fold.at[two_heads(to)], recv_a.at[d]), (dtot, dec_a.at[d])]):
            copy = pltpu.make_async_remote_copy(
                src_ref=src, dst_ref=dst, send_sem=a_send.at[d, n], recv_sem=a_recv.at[d, n],
                device_id=(4 * z + to, hd), device_id_type=MESH,
            )
            copy.start()
            a_copies.append(copy)
    recv_a[0] = fold[two_heads(j), :]
    dec_a[0] = dtot[...]
    for item in HALO_AFTER_A:
        halo(*item).start()

    acc[...] = jnp.zeros_like(acc)
    loads[2].wait()
    tri = rows_of((256, 256)) >= lanes((256, 256))

    def intra(h, _):
        start, low = head_window(h)
        window = pl.ds(start, WIN)
        mask = head_mask(low)
        keep = mask.astype(F32).astype(BF16)
        qw = q1[:, window] * keep
        kw = k1[:, window]
        vw = v1[:, window]
        s0 = dot(qw[:256], kw[:256], 1, 1)
        s1 = dot(qw[256:], kw, 1, 1)
        ci = crow[h]
        ci = jnp.concatenate([ci, ci], axis=1)
        cj = ct[pl.ds(h, 1), :]
        e0 = jnp.exp(jnp.where(tri, ci[:256] - cj[:, :256], NEG))
        e10 = jnp.exp(ci[256:] - cj[:, :256])
        e11 = jnp.exp(jnp.where(tri, ci[256:] - cj[:, 256:], NEG))
        m0 = (s0 * e0).astype(BF16)
        m1 = (s1 * jnp.concatenate([e10, e11], axis=1)).astype(BF16)
        acc[pl.ds(0, 256), window] = jnp.where(mask, dot(m0, vw[:256], 1, 0), acc[pl.ds(0, 256), window])
        acc[pl.ds(256, 256), window] = jnp.where(mask, dot(m1, vw, 1, 0), acc[pl.ds(256, 256), window])
        return 0

    lax.fori_loop(0, NH // 2, intra, 0)

    for copy in a_copies:
        copy.wait_recv()

    def member(i):
        return lax.rem(j + 4 - i, 4)

    def head_rows(hh):
        return slice(DH * hh, DH * hh + DH)

    for hh in range(2):
        total = jnp.zeros((DH, 128), F32)
        for i in range(4):
            decay = jnp.exp(dec_a[member(i), pl.ds(2 * j + hh, 1), :])
            total = decay * total + recv_a[member(i), head_rows(hh), :].astype(F32)
        tot_b[head_rows(hh), :] = total.astype(BF16)
    dec_s[...] = dec_a[0] + dec_a[1] + dec_a[2] + dec_a[3]
    b_copies = []
    for d in range(1, 8):
        pair = []
        for n, (src, dst) in enumerate([(tot_b, recv_b.at[d]), (dec_s, dec_b.at[d])]):
            pair.append(
                pltpu.make_async_remote_copy(
                    src_ref=src, dst_ref=dst, send_sem=b_send.at[d, n], recv_sem=b_recv.at[d, n],
                    device_id=(lax.rem(t + 4 * d, 32), hd), device_id_type=MESH,
                )
            )
        b_copies.append(pair)

        @pl.when(z + d < 8)
        def _(pair=pair):
            for copy in pair:
                copy.start()

    for item in HALO_AFTER_B:
        halo(*item).start()

    lax.fori_loop(NH // 2, NH, intra, 0)

    for d in range(1, 8):

        @pl.when(z >= d)
        def _(pair=b_copies[d - 1]):
            for copy in pair:
                copy.wait_recv()

    pacc[...] = jnp.zeros_like(pacc)
    for zz in range(7):

        @pl.when(zz < z)
        def _(zz=zz):
            slot = lax.rem(z + 8 - zz, 8)
            for hh in range(2):
                decay = jnp.exp(dec_b[slot, pl.ds(2 * j + hh, 1), :])
                pacc[head_rows(hh), :] = decay * pacc[head_rows(hh), :] + recv_b[slot, head_rows(hh), :].astype(F32)

    for hh in range(2):
        state = pacc[head_rows(hh), :]
        for i in range(4):
            send_c[i, head_rows(hh), :] = state.astype(BF16)
            decay = jnp.exp(dec_a[member(i), pl.ds(2 * j + hh, 1), :])
            state = decay * state + recv_a[member(i), head_rows(hh), :].astype(F32)
    c_copies = []
    for d in (1, 2, 3):
        to = lax.rem(j + d, 4)
        copy = pltpu.make_async_remote_copy(
            src_ref=send_c.at[to], dst_ref=recv_c.at[j], send_sem=c_send.at[d], recv_sem=c_recv.at[d],
            device_id=(4 * z + to, hd), device_id_type=MESH,
        )
        copy.start()
        c_copies.append(copy)
    recv_c[j] = send_c[j]
    for item in HALO_AFTER_C:
        halo(*item).start()
    loads[6].wait()
    for copy in c_copies:
        copy.wait_recv()

    for g in range(2):
        states = jnp.concatenate([recv_c[2 * g], recv_c[2 * g + 1]], axis=0).astype(F32)
        wide = jnp.concatenate([jnp.where(same_head(i), states, 0.0).astype(BF16) for i in range(3)], axis=1)
        ones = jnp.concatenate([same_head(i).astype(F32).astype(BF16) for i in range(3)], axis=1)
        both = dot(q1[:, half(g)], wide, 1, 0) * jnp.exp(cexp[:, half(g)]) + acc[:, half(g)]
        square = both * both
        high = square.astype(BF16)
        rest = (square - high.astype(F32)).astype(BF16)
        mean = (dot(high, ones, 1, 0) + dot(rest, ones, 1, 0)) * (1.0 / DH)
        normed[:, half(g)] = (both * lax.rsqrt(mean + EPS)).astype(BF16)

    left, right = pl.ds(0, HALF), pl.ds(HALF, HALF)

    def project(d, cols):
        xt = lax.rem(x + d, 4)
        a = jnp.concatenate(
            [
                normed[pl.ds(pl.multiple_of(64 * xt, 64), 64), :],
                normed[pl.ds(pl.multiple_of(256 + 64 * xt, 64), 64), :],
            ],
            axis=0,
        )
        return dot(a, w[:, cols], 1, 0)

    def x_copy(n, src, dst, to):
        return pltpu.make_async_remote_copy(
            src_ref=src, dst_ref=dst, send_sem=x_send.at[n], recv_sem=x_recv.at[n],
            device_id=(t, to), device_id_type=MESH,
        )

    x1 = [x_copy(0, x1s.at[0], x1r.at[0], x_up), x_copy(1, x1s.at[1], x1r.at[1], x_down)]
    x2a = [
        x_copy(2, x2s.at[0, :, right], x2r.at[0, :, right], x_up),
        x_copy(3, x2s.at[1, :, left], x2r.at[1, :, left], x_down),
    ]
    x2b = [
        x_copy(4, x2s.at[0, :, left], x2r.at[0, :, left], x_up),
        x_copy(5, x2s.at[1, :, right], x2r.at[1, :, right], x_down),
    ]
    step = 512

    def cols_at(i):
        return pl.ds(pl.multiple_of(step * i, step), step)

    for side in range(2):

        def opposite(i, _, side=side):
            x1s[side, :, cols_at(i)] = project(2, cols_at(i + 3 * side)).astype(BF16)
            return 0

        lax.fori_loop(0, 3, opposite, 0)
        x1[side].start()
    for side in range(2):

        def alone(i, _, side=side):
            cols = cols_at(i + 3 * (1 - side))
            x2s[side, :, cols] = project(1 + 2 * side, cols).astype(BF16)
            return 0

        lax.fori_loop(0, 3, alone, 0)
        x2a[side].start()
    for side in range(2):

        def kept(i, _, side=side):
            part[1 + side, :, cols_at(i)] = project(1 + 2 * side, cols_at(i + 3 * side))
            return 0

        lax.fori_loop(0, 3, kept, 0)

    def own_rows(i, _):
        value = project(0, cols_at(i))
        part[3 + lax.div(i, 3), :, cols_at(lax.rem(i, 3))] = value
        return 0

    lax.fori_loop(0, 6, own_rows, 0)

    def second_step():
        for side in range(2):
            x1[side].wait_recv()

            def add(i, _, side=side):
                total = part[1 + side, :, cols_at(i)] + x1r[side, :, cols_at(i)].astype(F32)
                x2s[side, :, cols_at(i + 3 * side)] = total.astype(BF16)
                return 0

            lax.fori_loop(0, 3, add, 0)
            x2b[side].start()

    y_copies = [
        pltpu.make_async_remote_copy(
            src_ref=ys.at[i], dst_ref=yr.at[i], send_sem=y_send.at[i], recv_sem=y_recv.at[i],
            device_id=(t, y_other), device_id_type=MESH,
        )
        for i in range(2)
    ]
    mine_rows = pl.ds(pl.multiple_of(64 * yl, 64), 64)
    their_rows = pl.ds(pl.multiple_of(64 * (1 - yl), 64), 64)

    def third_step():
        for i in range(2):
            if i == 0:
                x2b[0].wait_recv()
                x2a[1].wait_recv()
            else:
                x2a[0].wait_recv()
                x2b[1].wait_recv()

            def add(n, _, i=i):
                cols = cols_at(n + 3 * i)

                def total(rows):
                    return (
                        part[3 + i, rows, cols_at(n)]
                        + x2r[0, rows, cols].astype(F32)
                        + x2r[1, rows, cols].astype(F32)
                    )

                ys[i, :, cols_at(n)] = total(their_rows).astype(BF16)
                part[3 + i, mine_rows, cols_at(n)] = total(mine_rows)
                return 0

            lax.fori_loop(0, 3, add, 0)
            y_copies[i].start()

    def pass_on(g):
        for kv in range(2):
            arrived(1, kv, g).wait_recv()
            forward(kv, g).start()

    def need(g):
        for kv in range(2):
            for slot in (0, 2):
                arrived(slot, kv, g).wait_recv()

    scale = (1.0 / math.sqrt(DH)) * math.log2(math.e)
    upper = lanes((256, 256)) > rows_of((256, 256))

    def attend(h, _):
        start, low = head_window(h)
        window = pl.ds(start, WIN)
        mask = head_mask(low)
        keep = mask.astype(F32).astype(BF16)
        for i in range(2):
            keys = pl.ds(256 * i, SPAN)
            qw = q2[pl.ds(256 * i, 256), window] * keep
            s_scr[i] = dot(qw, kk[keys, window], 1, 1)
            tops = []
            for n in range(7):
                cols = pl.ds(256 * n, 256)
                if n == 0:
                    s_scr[i, :, cols] = jnp.where(upper, s_scr[i, :, cols], NEG)
                if n == 6:
                    s_scr[i, :, cols] = jnp.where(tri, s_scr[i, :, cols], NEG)
                block = s_scr[i, :, cols]
                top = jnp.maximum(block[:, :128], block[:, 128:])
                first = 3 - (i + n) // 2
                if first > 0:
                    top = jnp.minimum(top, jnp.where(t >= first, 1e38, -1e38))
                tops.append(top)
            while len(tops) > 1:
                tops = [jnp.maximum(*tops[n : n + 2]) if n + 1 < len(tops) else tops[n] for n in range(0, len(tops), 2)]
            peak = jnp.max(tops[0], axis=1, keepdims=True) * scale
            total = jnp.zeros((256, 128), F32)
            for n in range(7):
                cols = pl.ds(256 * n, 256)
                first = 3 - (i + n) // 2
                shift = peak + jnp.where(t >= first, 0.0, 1e30) if first > 0 else peak
                e = jnp.exp2(s_scr[i, :, cols] * scale - shift)
                total += e[:, :128] + e[:, 128:]
                p_scr[i, :, cols] = e.astype(BF16)
            out = dot(p_scr[i], vv[keys, window], 1, 0) * (1.0 / jnp.sum(total, axis=1, keepdims=True))
            rows = pl.ds(256 * i, 256)
            old = att_out[rows, window].astype(F32)
            att_out[rows, window] = jnp.where(mask, out, old).astype(BF16)
        return 0

    att_out[...] = jnp.zeros_like(att_out)
    for i in (3, 4, 5):
        loads[i].wait()
    pass_on(0)
    need(0)
    lax.fori_loop(0, 2, attend, 0)
    second_step()
    lax.fori_loop(2, 4, attend, 0)
    pass_on(1)
    need(1)
    lax.fori_loop(4, 6, attend, 0)
    third_step()
    lax.fori_loop(6, 8, attend, 0)

    for i in range(2):
        y_copies[i].wait_recv()
        for n in range(3):
            cols = pl.ds(step * n, step)
            total = part[3 + i, mine_rows, cols] + yr[i, :, cols].astype(F32)
            lin_out[:, pl.ds(HALF * i + step * n, step)] = total.astype(BF16)

    for item in HALO_FIRST + HALO_AFTER_A + HALO_AFTER_B + HALO_AFTER_C:
        halo(*item).wait_send()
    for g in range(2):
        for kv in range(2):
            forward(kv, g).wait_send()
    for copy in a_copies + c_copies + x1 + x2a + x2b + y_copies:
        copy.wait_send()
    for d in range(1, 8):

        @pl.when(z + d < 8)
        def _(pair=b_copies[d - 1]):
            for copy in pair:
                copy.wait_send()


def per_device(query1, key1, value1, log_decay, out_weight, query2, key2, value2):
    vm = pltpu.VMEM
    dma = pltpu.SemaphoreType.DMA
    hbm = pl.BlockSpec(memory_space=HBM)
    vmem = pl.BlockSpec(memory_space=vm)
    return pl.pallas_call(
        kernel,
        out_shape=(
            jax.ShapeDtypeStruct((64, PROJ), BF16),
            jax.ShapeDtypeStruct((ROWS, COLS), BF16),
        ),
        in_specs=[hbm, hbm, hbm, vmem, hbm, hbm, hbm, hbm],
        out_specs=(vmem, vmem),
        scratch_shapes=[
            vm((ROWS, COLS), BF16),
            vm((ROWS, COLS), BF16),
            vm((ROWS, COLS), BF16),
            vm((ROWS, COLS), BF16),
            vm((4 * ROWS, COLS), BF16),
            vm((4 * ROWS, COLS), BF16),
            vm((COLS, PROJ), BF16),
            vm((ROWS, 128), F32),
            vm((NH, ROWS, 128), F32),
            vm((NH, ROWS), F32),
            vm((ROWS, COLS), F32),
            vm((ROWS, COLS), F32),
            vm((COLS, 128), BF16),
            vm((NH, 128), F32),
            vm((4, 192, 128), BF16),
            vm((4, NH, 128), F32),
            vm((192, 128), BF16),
            vm((NH, 128), F32),
            vm((8, 192, 128), BF16),
            vm((8, NH, 128), F32),
            vm((192, 128), F32),
            vm((4, 192, 128), BF16),
            vm((4, 192, 128), BF16),
            vm((ROWS, COLS), BF16),
            vm((5, 128, HALF), F32),
            vm((2, 128, HALF), BF16),
            vm((2, 128, HALF), BF16),
            vm((2, 128, PROJ), BF16),
            vm((2, 128, PROJ), BF16),
            vm((2, 64, HALF), BF16),
            vm((2, 64, HALF), BF16),
            vm((2, 256, SPAN), F32),
            vm((2, 256, SPAN), BF16),
            dma((7,)),
            dma((2, 2, 2)),
            dma((3, 2, 2)),
            dma((2, 2)),
            dma((4, 2)),
            dma((4, 2)),
            dma((8, 2)),
            dma((8, 2)),
            dma((4,)),
            dma((4,)),
            dma((6,)),
            dma((6,)),
            dma((2,)),
            dma((2,)),
        ],
        compiler_params=pltpu.CompilerParams(
            collective_id=0, has_side_effects=True, vmem_limit_bytes=60 * 1024 * 1024
        ),
    )(query1, key1, value1, log_decay, out_weight, query2, key2, value2)


def solution(mesh):
    spec = P("ctx", "head")
    return jax.shard_map(
        per_device,
        mesh=mesh,
        in_specs=(spec, spec, spec, spec, P("head", None), spec, spec, spec),
        out_specs=(P(("ctx", "head"), None), spec),
        check_vma=False,
    )
```

```python
import math

import jax
import jax.numpy as jnp
from jax import lax
from jax.experimental import pallas as pl
from jax.experimental.pallas import tpu as pltpu
from jax.sharding import PartitionSpec as P

DH = 96
ROWS = 512
COLS = 768
NH = 8
GW = 384
PROJ = 3072
WIN = 256
SPAN = 1792
NEG = -1e30
EPS = 1e-6
MESH = pl.DeviceIdType.MESH
F32 = jnp.float32
BF16 = jnp.bfloat16
HBM = pltpu.MemorySpace.HBM

HALO_AFTER_A = [(0, 1, 0), (1, 0, 0)]
HALO_AFTER_B = [(1, 1, 0)]
HALO_AFTER_C = [(0, 0, 0), (0, 1, 1), (1, 0, 1), (0, 0, 1), (1, 1, 1)]
MSG = 112
STEP = 512


def dot(a, b, ca, cb):
    return lax.dot_general(a, b, (((ca,), (cb,)), ((), ())), preferred_element_type=F32)


def lanes(shape):
    return lax.broadcasted_iota(jnp.int32, shape, len(shape) - 1)


def rows_of(shape):
    return lax.broadcasted_iota(jnp.int32, shape, len(shape) - 2)


def head_window(h):
    start = GW * lax.div(h, 4) + 128 * lax.div(lax.rem(h, 4), 2)
    return pl.multiple_of(start, 128), DH * h - start


def head_mask(low):
    lane = lanes((1, WIN))
    return (lane >= low) & (lane < low + DH)


def same_head(tile):
    row = lax.div(rows_of((GW, 128)), DH)
    col = lax.div(lanes((GW, 128)) + 128 * tile, DH)
    return row == col


def kernel(
    q1h, k1h, v1h, dec, wh, q2h, k2h, v2h,
    lin_out, att_out,
    q1, k1, v1, q2, kk, vv, w,
    crow, ct, cexp, acc, fold, recv_a, tot_b, recv_b, pacc, send_c, recv_c,
    normed, own_part, pass_part, x1s, x1r, x2s, x2r, ys, yr,
    s_scr, p_scr,
    load_sem, halo_send, halo_recv, fwd_send, relay_send, a_send, a_recv, b_send, b_recv, c_send, c_recv,
    x1_send, x1_recv, x2_send, x2_recv, y_send, y_recv,
):
    t, hd = lax.axis_index("ctx"), lax.axis_index("head")
    core, y_hi = lax.rem(t, 2), lax.rem(lax.div(t, 2), 2)
    group, me = lax.div(t, 8), lax.rem(t, 8)
    yl, x = lax.div(hd, 4), lax.rem(hd, 4)
    sibling = t + 1 - 2 * core
    x_to = (yl * 4 + lax.rem(x + 1, 4), yl * 4 + lax.rem(x + 3, 4))
    y_other = (1 - yl) * 4 + x

    related = [
        (lax.rem(t + 2, 32), hd),
        (lax.rem(t + 30, 32), hd),
        (lax.rem(t + 4, 32), hd),
        (lax.rem(t + 28, 32), hd),
        (lax.rem(t + 29 + 6 * core, 32), hd),
        (t, x_to[0]),
        (t, x_to[1]),
        (t, y_other),
    ]
    related += [(8 * group + lax.rem(me + d, 8), hd) for d in range(1, 8)]
    related += [(lax.rem(t + 8 * d, 32), hd) for d in range(1, 4)]
    barrier = pltpu.get_barrier_semaphore()
    for device in related:
        pl.semaphore_signal(barrier, inc=1, device_id=device, device_id_type=MESH)

    own = pl.ds(3 * ROWS, ROWS)
    loads = [
        pltpu.make_async_copy(src, dst, load_sem.at[i])
        for i, (src, dst) in enumerate(
            [(k1h, k1), (v1h, v1), (q1h, q1), (q2h, q2), (k2h, kk.at[own]), (v2h, vv.at[own]), (wh, w)]
        )
    ]
    for copy in loads:
        copy.start()

    def half(g):
        return pl.ds(GW * g, GW)

    def block(slot):
        return pl.ds(pl.multiple_of(slot * ROWS, ROWS), ROWS)

    def halo(kind, kv, g):
        src, dst = ((k2h, kk), (v2h, vv))[kv]
        if kind == 1:
            slot, sem, target = 2 - 2 * core, 2 - 2 * core, lax.rem(t + 1 + 2 * core, 32)
        elif kv == 1:
            slot, sem, target = 1 + 3 * y_hi, 1 + 2 * y_hi, t + 2 - 4 * y_hi
        else:
            slot, sem, target = 1, 1, lax.rem(t + 2, 32)
        return pltpu.make_async_remote_copy(
            src_ref=src.at[:, half(g)],
            dst_ref=dst.at[block(slot), half(g)],
            send_sem=halo_send.at[kind, kv, g],
            recv_sem=halo_recv.at[sem, kv, g],
            device_id=(target, hd),
            device_id_type=MESH,
        )

    def arrived(sem, kv, g):
        dst = (kk, vv)[kv].at[pl.ds((4 if sem == 3 else sem) * ROWS, ROWS), half(g)]
        return pltpu.make_async_remote_copy(
            src_ref=dst,
            dst_ref=dst,
            send_sem=halo_send.at[0, kv, g],
            recv_sem=halo_recv.at[sem, kv, g],
            device_id=(sibling, hd),
            device_id_type=MESH,
        )

    def forward(kv, g):
        buf = (kk, vv)[kv]
        return pltpu.make_async_remote_copy(
            src_ref=buf.at[pl.ds(ROWS, ROWS), half(g)],
            dst_ref=buf.at[block(2 * core), half(g)],
            send_sem=fwd_send.at[kv, g],
            recv_sem=halo_recv.at[2 * core, kv, g],
            device_id=(sibling, hd),
            device_id_type=MESH,
        )

    def relay(g):
        return pltpu.make_async_remote_copy(
            src_ref=vv.at[pl.ds(4 * ROWS, ROWS), half(g)],
            dst_ref=vv.at[pl.ds(ROWS, ROWS), half(g)],
            send_sem=relay_send.at[g],
            recv_sem=halo_recv.at[1, 1, g],
            device_id=(lax.rem(t + 4, 32), hd),
            device_id_type=MESH,
        )

    def relay_on(g):
        @pl.when(y_hi == 0)
        def _():
            arrived(3, 1, g).wait_recv()
            relay(g).start()

    ct[...] = lax.dot_general(
        dec[...],
        (rows_of((ROWS, ROWS)) <= lanes((ROWS, ROWS))).astype(F32),
        (((1,), (0,)), ((), ())),
        precision=lax.Precision.HIGHEST,
        preferred_element_type=F32,
    )
    running = jnp.transpose(jnp.concatenate([ct[...], jnp.zeros((128 - NH, ROWS), F32)], axis=0))
    for h in range(NH):
        crow[h] = jnp.broadcast_to(running[:, h : h + 1], (ROWS, 128))
    lane = lanes((ROWS, 128))
    for g in range(2):
        for tile, cut in enumerate((96, 64, 32)):
            h = 4 * g + tile
            at = pl.ds(GW * g + 128 * tile, 128)
            cexp[:, at] = jnp.where(lane < cut, crow[h], crow[h + 1])

    def message(ref, index, state, decay):
        ref[index, :DH, :] = state.astype(BF16)
        high = decay.astype(BF16)
        rest = decay - high.astype(F32)
        middle = rest.astype(BF16)
        low = (rest - middle.astype(F32)).astype(BF16)
        row = rows_of((MSG - DH, 128))
        parts = [jnp.broadcast_to(p.astype(F32), (MSG - DH, 128)) for p in (high, middle, low)]
        tail = jnp.where(row == 0, parts[0], jnp.where(row == 1, parts[1], jnp.where(row == 2, parts[2], 0.0)))
        ref[index, DH:, :] = tail.astype(BF16)

    def decay_in(ref, index):
        return jnp.sum(ref[index, DH:, :].astype(F32), axis=0, keepdims=True)

    loads[0].wait()
    loads[1].wait()
    for g in range(2):
        c = cexp[:, half(g)]
        kw = (k1[:, half(g)].astype(F32) * jnp.exp(cexp[ROWS - 1 : ROWS, half(g)] - c)).astype(BF16)
        full = dot(kw, v1[:, half(g)], 0, 0)
        total = jnp.zeros((GW, 128), F32)
        for tile in range(3):
            total += jnp.where(same_head(tile), full[:, 128 * tile : 128 * tile + 128], 0.0)
        for i in range(4):
            h = 4 * g + i
            message(fold, h, total[DH * i : DH * i + DH], crow[h, ROWS - 1 : ROWS, :])

    pl.semaphore_wait(barrier, len(related))

    a_copies = []
    for d in range(1, 8):
        to = lax.rem(me + d, 8)
        copy = pltpu.make_async_remote_copy(
            src_ref=fold.at[to], dst_ref=recv_a.at[d], send_sem=a_send.at[d], recv_sem=a_recv.at[d],
            device_id=(8 * group + to, hd), device_id_type=MESH,
        )
        copy.start()
        a_copies.append(copy)
    recv_a[0] = fold[me]
    for item in HALO_AFTER_A:
        halo(*item).start()

    acc[...] = jnp.zeros_like(acc)
    loads[2].wait()
    tri = rows_of((256, 256)) >= lanes((256, 256))

    def intra(h, _):
        start, low = head_window(h)
        window = pl.ds(start, WIN)
        mask = head_mask(low)
        keep = mask.astype(F32).astype(BF16)
        qw = q1[:, window] * keep
        kw = k1[:, window]
        vw = v1[:, window]
        s0 = dot(qw[:256], kw[:256], 1, 1)
        s1 = dot(qw[256:], kw, 1, 1)
        ci = crow[h]
        ci = jnp.concatenate([ci, ci], axis=1)
        cj = ct[pl.ds(h, 1), :]
        e0 = jnp.exp(jnp.where(tri, ci[:256] - cj[:, :256], NEG))
        e10 = jnp.exp(ci[256:] - cj[:, :256])
        e11 = jnp.exp(jnp.where(tri, ci[256:] - cj[:, 256:], NEG))
        m0 = (s0 * e0).astype(BF16)
        m1 = (s1 * jnp.concatenate([e10, e11], axis=1)).astype(BF16)
        acc[pl.ds(0, 256), window] = jnp.where(mask, dot(m0, vw[:256], 1, 0), acc[pl.ds(0, 256), window])
        acc[pl.ds(256, 256), window] = jnp.where(mask, dot(m1, vw, 1, 0), acc[pl.ds(256, 256), window])
        return 0

    lax.fori_loop(0, NH // 2, intra, 0)

    for copy in a_copies:
        copy.wait_recv()

    def member(i):
        return lax.rem(me + 8 - i, 8)

    def then(state, ref, index):
        return jnp.exp(decay_in(ref, index)) * state + ref[index, :DH, :].astype(F32)

    total = jnp.zeros((DH, 128), F32)
    decay = jnp.zeros((1, 128), F32)
    for i in range(8):
        total = then(total, recv_a, member(i))
        decay = decay + decay_in(recv_a, i)
    message(tot_b, 0, total, decay)
    b_copies = []
    for d in range(1, 4):
        copy = pltpu.make_async_remote_copy(
            src_ref=tot_b.at[0], dst_ref=recv_b.at[d], send_sem=b_send.at[d], recv_sem=b_recv.at[d],
            device_id=(lax.rem(t + 8 * d, 32), hd), device_id_type=MESH,
        )
        b_copies.append(copy)

        @pl.when(group + d < 4)
        def _(copy=copy):
            copy.start()

    for item in HALO_AFTER_B:
        halo(*item).start()

    lax.fori_loop(NH // 2, NH, intra, 0)

    pacc[...] = jnp.zeros_like(pacc)
    for d in range(3, 0, -1):

        @pl.when(group >= d)
        def _(d=d):
            b_copies[d - 1].wait_recv()
            pacc[...] = then(pacc[...], recv_b, d)

    state = pacc[...]
    for i in range(8):
        send_c[i] = state.astype(BF16)
        if i < 7:
            state = then(state, recv_a, member(i))
    c_copies = []
    for d in range(1, 8):
        to = lax.rem(me + d, 8)
        copy = pltpu.make_async_remote_copy(
            src_ref=send_c.at[to], dst_ref=recv_c.at[me], send_sem=c_send.at[d], recv_sem=c_recv.at[d],
            device_id=(8 * group + to, hd), device_id_type=MESH,
        )
        copy.start()
        c_copies.append(copy)
    recv_c[me] = send_c[me]
    for item in HALO_AFTER_C:
        halo(*item).start()
    loads[6].wait()
    relay_on(0)
    for copy in c_copies:
        copy.wait_recv()

    for g in range(2):
        states = jnp.concatenate([recv_c[4 * g + i] for i in range(4)], axis=0).astype(F32)
        wide = jnp.concatenate([jnp.where(same_head(i), states, 0.0).astype(BF16) for i in range(3)], axis=1)
        ones = jnp.concatenate([same_head(i).astype(F32).astype(BF16) for i in range(3)], axis=1)
        both = dot(q1[:, half(g)], wide, 1, 0) * jnp.exp(cexp[:, half(g)]) + acc[:, half(g)]
        square = both * both
        high = square.astype(BF16)
        rest = (square - high.astype(F32)).astype(BF16)
        mean = (dot(high, ones, 1, 0) + dot(rest, ones, 1, 0)) * (1.0 / DH)
        normed[:, half(g)] = (both * lax.rsqrt(mean + EPS)).astype(BF16)

    def cols_at(i):
        return pl.ds(pl.multiple_of(STEP * i, STEP), STEP)

    def project(d, i):
        xt = lax.rem(x + d, 4)
        a = jnp.concatenate(
            [
                normed[pl.ds(pl.multiple_of(64 * xt, 64), 64), :],
                normed[pl.ds(pl.multiple_of(256 + 64 * xt, 64), 64), :],
            ],
            axis=0,
        )
        return dot(a, w[:, cols_at(i)], 1, 0)

    def x1(side, c):
        return pltpu.make_async_remote_copy(
            src_ref=x1s.at[side, c], dst_ref=x1r.at[side, c], send_sem=x1_send.at[side, c], recv_sem=x1_recv.at[side, c],
            device_id=(t, x_to[side]), device_id_type=MESH,
        )

    def x2(to, i):
        return pltpu.make_async_remote_copy(
            src_ref=x2s.at[to, i], dst_ref=x2r.at[to, i], send_sem=x2_send.at[to, i], recv_sem=x2_recv.at[to, i],
            device_id=(t, x_to[to]), device_id_type=MESH,
        )

    def yc(side, c):
        return pltpu.make_async_remote_copy(
            src_ref=ys.at[side, c], dst_ref=yr.at[side, c], send_sem=y_send.at[side, c], recv_sem=y_recv.at[side, c],
            device_id=(t, y_other), device_id_type=MESH,
        )

    def first(c, _):
        for side in range(2):
            x1s[side, c] = project(2, c + 3 * side).astype(BF16)
            x1(side, c).start()
        return 0

    def alone(c, _):
        for side in range(2):
            x2s[side, c + 3 - 3 * side] = project(1 + 2 * side, c + 3 - 3 * side).astype(BF16)
        return 0

    def kept(c, _):
        for side in range(2):
            pass_part[side, c] = project(1 + 2 * side, c + 3 * side)
        return 0

    def mine(i, _):
        own_part[i] = project(0, i)
        return 0

    lax.fori_loop(0, 3, first, 0)
    lax.fori_loop(0, 3, alone, 0)
    for side in range(2):
        x2(side, 3 - 3 * side).start()
    lax.fori_loop(0, 3, kept, 0)
    lax.fori_loop(0, 6, mine, 0)

    def second(c):
        for side in range(2):
            x1(side, c).wait_recv()
            x2s[side, c + 3 * side] = (pass_part[side, c] + x1r[side, c].astype(F32)).astype(BF16)
            x2(side, c + 3 * side).start()
        if c < 2:
            for side in range(2):
                x2(side, c + 1 + 3 - 3 * side).start()

    mine_rows = pl.ds(pl.multiple_of(64 * yl, 64), 64)
    their_rows = pl.ds(pl.multiple_of(64 * (1 - yl), 64), 64)

    def third(c):
        for side in range(2):
            i = c + 3 * side
            x2(0, i).wait_recv()
            x2(1, i).wait_recv()

            def total(rows):
                return own_part[i, rows] + x2r[0, i, rows].astype(F32) + x2r[1, i, rows].astype(F32)

            ys[side, c] = total(their_rows).astype(BF16)
            yc(side, c).start()
            own_part[i, mine_rows] = total(mine_rows)

    def last(c):
        for side in range(2):
            i = c + 3 * side
            yc(side, c).wait_recv()
            lin_out[:, pl.ds(STEP * i, STEP)] = (own_part[i, mine_rows] + yr[side, c].astype(F32)).astype(BF16)

    def pass_on(g):
        for kv in range(2):
            arrived(1, kv, g).wait_recv()
            forward(kv, g).start()

    def need(g):
        for kv in range(2):
            for slot in (0, 2):
                arrived(slot, kv, g).wait_recv()

    scale = (1.0 / math.sqrt(DH)) * math.log2(math.e)
    upper = lanes((256, 256)) > rows_of((256, 256))

    def attend(h, _):
        start, low = head_window(h)
        window = pl.ds(start, WIN)
        mask = head_mask(low)
        keep = mask.astype(F32).astype(BF16)
        for i in range(2):
            keys = pl.ds(256 * i, SPAN)
            qw = q2[pl.ds(256 * i, 256), window] * keep
            s_scr[i] = dot(qw, kk[keys, window], 1, 1)
            tops = []
            for n in range(7):
                cols = pl.ds(256 * n, 256)
                if n == 0:
                    s_scr[i, :, cols] = jnp.where(upper, s_scr[i, :, cols], NEG)
                if n == 6:
                    s_scr[i, :, cols] = jnp.where(tri, s_scr[i, :, cols], NEG)
                block = s_scr[i, :, cols]
                top = jnp.maximum(block[:, :128], block[:, 128:])
                first = 3 - (i + n) // 2
                if first > 0:
                    top = jnp.minimum(top, jnp.where(t >= first, 1e38, -1e38))
                tops.append(top)
            while len(tops) > 1:
                tops = [jnp.maximum(*tops[n : n + 2]) if n + 1 < len(tops) else tops[n] for n in range(0, len(tops), 2)]
            peak = jnp.max(tops[0], axis=1, keepdims=True) * scale
            total = jnp.zeros((256, 128), F32)
            for n in range(7):
                cols = pl.ds(256 * n, 256)
                first = 3 - (i + n) // 2
                shift = peak + jnp.where(t >= first, 0.0, 1e30) if first > 0 else peak
                e = jnp.exp2(s_scr[i, :, cols] * scale - shift)
                total += e[:, :128] + e[:, 128:]
                p_scr[i, :, cols] = e.astype(BF16)
            out = dot(p_scr[i], vv[keys, window], 1, 0) * (1.0 / jnp.sum(total, axis=1, keepdims=True))
            rows = pl.ds(256 * i, 256)
            old = att_out[rows, window].astype(F32)
            att_out[rows, window] = jnp.where(mask, out, old).astype(BF16)
        return 0

    att_out[...] = jnp.zeros_like(att_out)
    for i in (3, 4, 5):
        loads[i].wait()
    pass_on(0)
    need(0)
    lax.fori_loop(0, 1, attend, 0)
    second(0)
    lax.fori_loop(1, 3, attend, 0)
    second(1)
    relay_on(1)
    lax.fori_loop(3, 4, attend, 0)
    second(2)
    third(0)
    pass_on(1)
    need(1)
    lax.fori_loop(4, 5, attend, 0)
    third(1)
    lax.fori_loop(5, 7, attend, 0)
    third(2)
    last(0)
    lax.fori_loop(7, 8, attend, 0)
    last(1)
    last(2)

    for item in HALO_AFTER_A + HALO_AFTER_B + HALO_AFTER_C:
        halo(*item).wait_send()
    for g in range(2):
        for kv in range(2):
            forward(kv, g).wait_send()

        @pl.when(y_hi == 0)
        def _(g=g):
            relay(g).wait_send()

    for copy in a_copies + c_copies:
        copy.wait_send()
    for side in range(2):
        for c in range(3):
            x1(side, c).wait_send()
            yc(side, c).wait_send()
        for i in range(6):
            x2(side, i).wait_send()
    for d in range(1, 4):

        @pl.when(group + d < 4)
        def _(copy=b_copies[d - 1]):
            copy.wait_send()


def per_device(query1, key1, value1, log_decay, out_weight, query2, key2, value2):
    vm = pltpu.VMEM
    dma = pltpu.SemaphoreType.DMA
    hbm = pl.BlockSpec(memory_space=HBM)
    vmem = pl.BlockSpec(memory_space=vm)
    return pl.pallas_call(
        kernel,
        out_shape=(
            jax.ShapeDtypeStruct((64, PROJ), BF16),
            jax.ShapeDtypeStruct((ROWS, COLS), BF16),
        ),
        in_specs=[hbm, hbm, hbm, vmem, hbm, hbm, hbm, hbm],
        out_specs=(vmem, vmem),
        scratch_shapes=[
            vm((ROWS, COLS), BF16),
            vm((ROWS, COLS), BF16),
            vm((ROWS, COLS), BF16),
            vm((ROWS, COLS), BF16),
            vm((4 * ROWS, COLS), BF16),
            vm((5 * ROWS, COLS), BF16),
            vm((COLS, PROJ), BF16),
            vm((NH, ROWS, 128), F32),
            vm((NH, ROWS), F32),
            vm((ROWS, COLS), F32),
            vm((ROWS, COLS), F32),
            vm((NH, MSG, 128), BF16),
            vm((8, MSG, 128), BF16),
            vm((1, MSG, 128), BF16),
            vm((4, MSG, 128), BF16),
            vm((DH, 128), F32),
            vm((8, DH, 128), BF16),
            vm((8, DH, 128), BF16),
            vm((ROWS, COLS), BF16),
            vm((6, 128, STEP), F32),
            vm((2, 3, 128, STEP), F32),
            vm((2, 3, 128, STEP), BF16),
            vm((2, 3, 128, STEP), BF16),
            vm((2, 6, 128, STEP), BF16),
            vm((2, 6, 128, STEP), BF16),
            vm((2, 3, 64, STEP), BF16),
            vm((2, 3, 64, STEP), BF16),
            vm((2, 256, SPAN), F32),
            vm((2, 256, SPAN), BF16),
            dma((7,)),
            dma((2, 2, 2)),
            dma((4, 2, 2)),
            dma((2, 2)),
            dma((2,)),
            dma((8,)),
            dma((8,)),
            dma((4,)),
            dma((4,)),
            dma((8,)),
            dma((8,)),
            dma((2, 3)),
            dma((2, 3)),
            dma((2, 6)),
            dma((2, 6)),
            dma((2, 3)),
            dma((2, 3)),
        ],
        compiler_params=pltpu.CompilerParams(
            collective_id=0, has_side_effects=True, vmem_limit_bytes=60 * 1024 * 1024
        ),
    )(query1, key1, value1, log_decay.T, out_weight, query2, key2, value2)


def solution(mesh):
    spec = P("ctx", "head")
    return jax.shard_map(
        per_device,
        mesh=mesh,
        in_specs=(spec, spec, spec, spec, P("head", None), spec, spec, spec),
        out_specs=(P(("ctx", "head"), None), spec),
        check_vma=False,
    )
```

```python
import math

import jax
import jax.numpy as jnp
from jax import lax
from jax.experimental import pallas as pl
from jax.experimental.pallas import tpu as pltpu
from jax.sharding import PartitionSpec as P

DH = 96
ROWS = 512
COLS = 768
NH = 8
GW = 384
PROJ = 3072
WIN = 256
SPAN = 1792
NEG = -1e30
EPS = 1e-6
MESH = pl.DeviceIdType.MESH
F32 = jnp.float32
BF16 = jnp.bfloat16
HBM = pltpu.MemorySpace.HBM

PIECES = ((0, 256, 0, 384), (256, 256, 0, 384), (0, 512, 384, 256), (0, 512, 640, 128))
HALO_AFTER_A = [(0, 1, 0), (1, 0, 0), (0, 1, 1), (1, 0, 1)]
HALO_AFTER_B = [(1, 1, 0), (0, 0, 0), (1, 1, 1)]
HALO_AFTER_C = [(0, 1, 2), (0, 1, 3), (1, 0, 2), (0, 0, 1), (1, 1, 2), (0, 0, 2), (1, 0, 3), (0, 0, 3), (1, 1, 3)]
VMEM_LIMIT = 60 * 1024 * 1024
MSG = 112
STEP = 512


def dot(a, b, ca, cb):
    return lax.dot_general(a, b, (((ca,), (cb,)), ((), ())), preferred_element_type=F32)


def lanes(shape):
    return lax.broadcasted_iota(jnp.int32, shape, len(shape) - 1)


def rows_of(shape):
    return lax.broadcasted_iota(jnp.int32, shape, len(shape) - 2)


def head_window(h):
    start = GW * lax.div(h, 4) + 128 * lax.div(lax.rem(h, 4), 2)
    return pl.multiple_of(start, 128), DH * h - start


def head_mask(low):
    lane = lanes((1, WIN))
    return (lane >= low) & (lane < low + DH)


def same_head(tile):
    row = lax.div(rows_of((GW, 128)), DH)
    col = lax.div(lanes((GW, 128)) + 128 * tile, DH)
    return row == col


def kernel(
    q1h, k1h, v1h, dec, wh, q2h, k2h, v2h,
    lin_out, att_out,
    q1, k1, v1, q2, kk, vv, w,
    crow, ct, cexp, acc, fold, recv_a, tot_b, recv_b, pacc, send_c, recv_c,
    normed, own_part, pass_part, x1s, x1r, x2s, x2r, ys, yr,
    s_scr, p_scr,
    load_sem, halo_send, halo_recv, fwd_send, relay_send, a_send, a_recv, b_send, b_recv, c_send, c_recv,
    x1_send, x1_recv, x2_send, x2_recv, y_send, y_recv,
):
    t, hd = lax.axis_index("ctx"), lax.axis_index("head")
    core, y_hi = lax.rem(t, 2), lax.rem(lax.div(t, 2), 2)
    group, me = lax.div(t, 8), lax.rem(t, 8)
    yl, x = lax.div(hd, 4), lax.rem(hd, 4)
    sibling = t + 1 - 2 * core
    x_to = (yl * 4 + lax.rem(x + 1, 4), yl * 4 + lax.rem(x + 3, 4))
    y_other = (1 - yl) * 4 + x

    related = [
        (lax.rem(t + 2, 32), hd),
        (lax.rem(t + 30, 32), hd),
        (lax.rem(t + 4, 32), hd),
        (lax.rem(t + 28, 32), hd),
        (lax.rem(t + 29 + 6 * core, 32), hd),
        (t, x_to[0]),
        (t, x_to[1]),
        (t, y_other),
    ]
    related += [(8 * group + lax.rem(me + d, 8), hd) for d in range(1, 8)]
    related += [(lax.rem(t + 8 * d, 32), hd) for d in range(1, 4)]
    barrier = pltpu.get_barrier_semaphore()
    for device in related:
        pl.semaphore_signal(barrier, inc=1, device_id=device, device_id_type=MESH)

    own = pl.ds(3 * ROWS, ROWS)
    loads = [
        pltpu.make_async_copy(src, dst, load_sem.at[i])
        for i, (src, dst) in enumerate(
            [(k1h, k1), (v1h, v1), (q1h, q1), (q2h, q2), (k2h, kk.at[own]), (v2h, vv.at[own]), (wh, w)]
        )
    ]
    for copy in loads:
        copy.start()

    def half(g):
        return pl.ds(GW * g, GW)

    def piece(slot, n):
        row, rows, col, cols = PIECES[n]
        return pl.ds(pl.multiple_of(slot * ROWS + row, 256), rows), pl.ds(col, cols)

    def halo(kind, kv, n):
        src, dst = ((k2h, kk), (v2h, vv))[kv]
        if kind == 1:
            slot, sem, target = 2 - 2 * core, 2 - 2 * core, lax.rem(t + 1 + 2 * core, 32)
        elif kv == 1:
            slot, sem, target = 1 + 3 * y_hi, 1 + 2 * y_hi, t + 2 - 4 * y_hi
        else:
            slot, sem, target = 1, 1, lax.rem(t + 2, 32)
        return pltpu.make_async_remote_copy(
            src_ref=src.at[piece(0, n)],
            dst_ref=dst.at[piece(slot, n)],
            send_sem=halo_send.at[kind, kv, n],
            recv_sem=halo_recv.at[sem, kv, n],
            device_id=(target, hd),
            device_id_type=MESH,
        )

    def arrived(sem, kv, n):
        dst = (kk, vv)[kv].at[piece(4 if sem == 3 else sem, n)]
        return pltpu.make_async_remote_copy(
            src_ref=dst,
            dst_ref=dst,
            send_sem=halo_send.at[0, kv, n],
            recv_sem=halo_recv.at[sem, kv, n],
            device_id=(sibling, hd),
            device_id_type=MESH,
        )

    def forward(kv, n):
        buf = (kk, vv)[kv]
        return pltpu.make_async_remote_copy(
            src_ref=buf.at[piece(1, n)],
            dst_ref=buf.at[piece(2 * core, n)],
            send_sem=fwd_send.at[kv, n],
            recv_sem=halo_recv.at[2 * core, kv, n],
            device_id=(sibling, hd),
            device_id_type=MESH,
        )

    def relay(n):
        return pltpu.make_async_remote_copy(
            src_ref=vv.at[piece(4, n)],
            dst_ref=vv.at[piece(1, n)],
            send_sem=relay_send.at[n],
            recv_sem=halo_recv.at[1, 1, n],
            device_id=(lax.rem(t + 4, 32), hd),
            device_id_type=MESH,
        )

    def relay_on(n):
        @pl.when(y_hi == 0)
        def _():
            arrived(3, 1, n).wait_recv()
            relay(n).start()

    ct[...] = lax.dot_general(
        dec[...],
        (rows_of((ROWS, ROWS)) <= lanes((ROWS, ROWS))).astype(F32),
        (((1,), (0,)), ((), ())),
        precision=lax.Precision.HIGHEST,
        preferred_element_type=F32,
    )
    running = jnp.transpose(jnp.concatenate([ct[...], jnp.zeros((128 - NH, ROWS), F32)], axis=0))
    for h in range(NH):
        crow[h] = jnp.broadcast_to(running[:, h : h + 1], (ROWS, 128))
    lane = lanes((ROWS, 128))
    for g in range(2):
        for tile, cut in enumerate((96, 64, 32)):
            h = 4 * g + tile
            at = pl.ds(GW * g + 128 * tile, 128)
            cexp[:, at] = jnp.where(lane < cut, crow[h], crow[h + 1])

    def message(ref, index, state, decay):
        ref[index, :DH, :] = state.astype(BF16)
        high = decay.astype(BF16)
        rest = decay - high.astype(F32)
        middle = rest.astype(BF16)
        low = (rest - middle.astype(F32)).astype(BF16)
        row = rows_of((MSG - DH, 128))
        parts = [jnp.broadcast_to(p.astype(F32), (MSG - DH, 128)) for p in (high, middle, low)]
        tail = jnp.where(row == 0, parts[0], jnp.where(row == 1, parts[1], jnp.where(row == 2, parts[2], 0.0)))
        ref[index, DH:, :] = tail.astype(BF16)

    def decay_in(ref, index):
        return jnp.sum(ref[index, DH:, :].astype(F32), axis=0, keepdims=True)

    loads[0].wait()
    loads[1].wait()
    for g in range(2):
        c = cexp[:, half(g)]
        kw = (k1[:, half(g)].astype(F32) * jnp.exp(cexp[ROWS - 1 : ROWS, half(g)] - c)).astype(BF16)
        full = dot(kw, v1[:, half(g)], 0, 0)
        total = jnp.zeros((GW, 128), F32)
        for tile in range(3):
            total += jnp.where(same_head(tile), full[:, 128 * tile : 128 * tile + 128], 0.0)
        for i in range(4):
            h = 4 * g + i
            message(fold, h, total[DH * i : DH * i + DH], crow[h, ROWS - 1 : ROWS, :])

    pl.semaphore_wait(barrier, len(related))

    a_copies = []
    for d in range(1, 8):
        to = lax.rem(me + d, 8)
        copy = pltpu.make_async_remote_copy(
            src_ref=fold.at[to], dst_ref=recv_a.at[d], send_sem=a_send.at[d], recv_sem=a_recv.at[d],
            device_id=(8 * group + to, hd), device_id_type=MESH,
        )
        copy.start()
        a_copies.append(copy)
    recv_a[0] = fold[me]
    for item in HALO_AFTER_A:
        halo(*item).start()

    acc[...] = jnp.zeros_like(acc)
    loads[2].wait()
    tri = rows_of((256, 256)) >= lanes((256, 256))

    def intra(h, _):
        start, low = head_window(h)
        window = pl.ds(start, WIN)
        mask = head_mask(low)
        keep = mask.astype(F32).astype(BF16)
        qw = q1[:, window] * keep
        kw = k1[:, window]
        vw = v1[:, window]
        s0 = dot(qw[:256], kw[:256], 1, 1)
        s1 = dot(qw[256:], kw, 1, 1)
        ci = crow[h]
        ci = jnp.concatenate([ci, ci], axis=1)
        cj = ct[pl.ds(h, 1), :]
        e0 = jnp.exp(jnp.where(tri, ci[:256] - cj[:, :256], NEG))
        e10 = jnp.exp(ci[256:] - cj[:, :256])
        e11 = jnp.exp(jnp.where(tri, ci[256:] - cj[:, 256:], NEG))
        m0 = (s0 * e0).astype(BF16)
        m1 = (s1 * jnp.concatenate([e10, e11], axis=1)).astype(BF16)
        acc[pl.ds(0, 256), window] = jnp.where(mask, dot(m0, vw[:256], 1, 0), acc[pl.ds(0, 256), window])
        acc[pl.ds(256, 256), window] = jnp.where(mask, dot(m1, vw, 1, 0), acc[pl.ds(256, 256), window])
        return 0

    lax.fori_loop(0, NH // 2, intra, 0)

    for copy in a_copies:
        copy.wait_recv()

    def member(i):
        return lax.rem(me + 8 - i, 8)

    def then(state, ref, index):
        return jnp.exp(decay_in(ref, index)) * state + ref[index, :DH, :].astype(F32)

    total = jnp.zeros((DH, 128), F32)
    decay = jnp.zeros((1, 128), F32)
    for i in range(8):
        total = then(total, recv_a, member(i))
        decay = decay + decay_in(recv_a, i)
    message(tot_b, 0, total, decay)
    b_copies = []
    for d in range(1, 4):
        copy = pltpu.make_async_remote_copy(
            src_ref=tot_b.at[0], dst_ref=recv_b.at[d], send_sem=b_send.at[d], recv_sem=b_recv.at[d],
            device_id=(lax.rem(t + 8 * d, 32), hd), device_id_type=MESH,
        )
        b_copies.append(copy)

        @pl.when(group + d < 4)
        def _(copy=copy):
            copy.start()

    for item in HALO_AFTER_B:
        halo(*item).start()

    lax.fori_loop(NH // 2, NH, intra, 0)

    pacc[...] = jnp.zeros_like(pacc)
    for d in range(3, 0, -1):

        @pl.when(group >= d)
        def _(d=d):
            b_copies[d - 1].wait_recv()
            pacc[...] = then(pacc[...], recv_b, d)

    state = pacc[...]
    for i in range(8):
        send_c[i] = state.astype(BF16)
        if i < 7:
            state = then(state, recv_a, member(i))
    c_copies = []
    for d in range(1, 8):
        to = lax.rem(me + d, 8)
        copy = pltpu.make_async_remote_copy(
            src_ref=send_c.at[to], dst_ref=recv_c.at[me], send_sem=c_send.at[d], recv_sem=c_recv.at[d],
            device_id=(8 * group + to, hd), device_id_type=MESH,
        )
        copy.start()
        c_copies.append(copy)
    recv_c[me] = send_c[me]
    for item in HALO_AFTER_C:
        halo(*item).start()
    loads[6].wait()
    relay_on(0)
    relay_on(1)
    for copy in c_copies:
        copy.wait_recv()

    for g in range(2):
        states = jnp.concatenate([recv_c[4 * g + i] for i in range(4)], axis=0).astype(F32)
        wide = jnp.concatenate([jnp.where(same_head(i), states, 0.0).astype(BF16) for i in range(3)], axis=1)
        ones = jnp.concatenate([same_head(i).astype(F32).astype(BF16) for i in range(3)], axis=1)
        both = dot(q1[:, half(g)], wide, 1, 0) * jnp.exp(cexp[:, half(g)]) + acc[:, half(g)]
        square = both * both
        high = square.astype(BF16)
        rest = (square - high.astype(F32)).astype(BF16)
        mean = (dot(high, ones, 1, 0) + dot(rest, ones, 1, 0)) * (1.0 / DH)
        normed[:, half(g)] = (both * lax.rsqrt(mean + EPS)).astype(BF16)

    def cols_at(i):
        return pl.ds(pl.multiple_of(STEP * i, STEP), STEP)

    def project(d, i):
        xt = lax.rem(x + d, 4)
        a = jnp.concatenate(
            [
                normed[pl.ds(pl.multiple_of(64 * xt, 64), 64), :],
                normed[pl.ds(pl.multiple_of(256 + 64 * xt, 64), 64), :],
            ],
            axis=0,
        )
        return dot(a, w[:, cols_at(i)], 1, 0)

    def x1(side, c):
        return pltpu.make_async_remote_copy(
            src_ref=x1s.at[side, c], dst_ref=x1r.at[side, c], send_sem=x1_send.at[side, c], recv_sem=x1_recv.at[side, c],
            device_id=(t, x_to[side]), device_id_type=MESH,
        )

    def x2(to, i):
        return pltpu.make_async_remote_copy(
            src_ref=x2s.at[to, i], dst_ref=x2r.at[to, i], send_sem=x2_send.at[to, i], recv_sem=x2_recv.at[to, i],
            device_id=(t, x_to[to]), device_id_type=MESH,
        )

    def yc(side, c):
        return pltpu.make_async_remote_copy(
            src_ref=ys.at[side, c], dst_ref=yr.at[side, c], send_sem=y_send.at[side, c], recv_sem=y_recv.at[side, c],
            device_id=(t, y_other), device_id_type=MESH,
        )

    def first(c, _):
        for side in range(2):
            x1s[side, c] = project(2, c + 3 * side).astype(BF16)
            x1(side, c).start()
        return 0

    def alone(c, _):
        for side in range(2):
            x2s[side, c + 3 - 3 * side] = project(1 + 2 * side, c + 3 - 3 * side).astype(BF16)
        return 0

    def kept(c, _):
        for side in range(2):
            pass_part[side, c] = project(1 + 2 * side, c + 3 * side)
        return 0

    def mine(i, _):
        own_part[i] = project(0, i)
        return 0

    lax.fori_loop(0, 3, first, 0)
    lax.fori_loop(0, 3, alone, 0)
    for side in range(2):
        x2(side, 3 - 3 * side).start()
    lax.fori_loop(0, 3, kept, 0)
    lax.fori_loop(0, 6, mine, 0)

    def second(c):
        for side in range(2):
            x1(side, c).wait_recv()
            x2s[side, c + 3 * side] = (pass_part[side, c] + x1r[side, c].astype(F32)).astype(BF16)
            x2(side, c + 3 * side).start()
        if c < 2:
            for side in range(2):
                x2(side, c + 1 + 3 - 3 * side).start()

    mine_rows = pl.ds(pl.multiple_of(64 * yl, 64), 64)
    their_rows = pl.ds(pl.multiple_of(64 * (1 - yl), 64), 64)

    def third(c):
        for side in range(2):
            i = c + 3 * side
            x2(0, i).wait_recv()
            x2(1, i).wait_recv()

            def total(rows):
                return own_part[i, rows] + x2r[0, i, rows].astype(F32) + x2r[1, i, rows].astype(F32)

            ys[side, c] = total(their_rows).astype(BF16)
            yc(side, c).start()
            own_part[i, mine_rows] = total(mine_rows)

    def last(c):
        for side in range(2):
            i = c + 3 * side
            yc(side, c).wait_recv()
            lin_out[:, pl.ds(STEP * i, STEP)] = (own_part[i, mine_rows] + yr[side, c].astype(F32)).astype(BF16)

    def pass_on(kv, n):
        arrived(1, kv, n).wait_recv()
        forward(kv, n).start()

    def need(n):
        for kv in range(2):
            for slot in (0, 2):
                arrived(slot, kv, n).wait_recv()

    scale = (1.0 / math.sqrt(DH)) * math.log2(math.e)
    upper = lanes((256, 256)) > rows_of((256, 256))

    def attend(h, _):
        start, low = head_window(h)
        window = pl.ds(start, WIN)
        mask = head_mask(low)
        keep = mask.astype(F32).astype(BF16)
        for i in range(2):
            keys = pl.ds(256 * i, SPAN)
            qw = q2[pl.ds(256 * i, 256), window] * keep
            s_scr[i] = dot(qw, kk[keys, window], 1, 1)
            tops = []
            for n in range(7):
                cols = pl.ds(256 * n, 256)
                if n == 0:
                    s_scr[i, :, cols] = jnp.where(upper, s_scr[i, :, cols], NEG)
                if n == 6:
                    s_scr[i, :, cols] = jnp.where(tri, s_scr[i, :, cols], NEG)
                block = s_scr[i, :, cols]
                top = jnp.maximum(block[:, :128], block[:, 128:])
                first = 3 - (i + n) // 2
                if first > 0:
                    top = jnp.minimum(top, jnp.where(t >= first, 1e38, -1e38))
                tops.append(top)
            while len(tops) > 1:
                tops = [jnp.maximum(*tops[n : n + 2]) if n + 1 < len(tops) else tops[n] for n in range(0, len(tops), 2)]
            peak = jnp.max(tops[0], axis=1, keepdims=True) * scale
            total = jnp.zeros((256, 128), F32)
            for n in range(7):
                cols = pl.ds(256 * n, 256)
                first = 3 - (i + n) // 2
                shift = peak + jnp.where(t >= first, 0.0, 1e30) if first > 0 else peak
                e = jnp.exp2(s_scr[i, :, cols] * scale - shift)
                total += e[:, :128] + e[:, 128:]
                p_scr[i, :, cols] = e.astype(BF16)
            out = dot(p_scr[i], vv[keys, window], 1, 0) * (1.0 / jnp.sum(total, axis=1, keepdims=True))
            rows = pl.ds(256 * i, 256)
            old = att_out[rows, window].astype(F32)
            att_out[rows, window] = jnp.where(mask, out, old).astype(BF16)
        return 0

    att_out[...] = jnp.zeros_like(att_out)
    for i in (3, 4, 5):
        loads[i].wait()
    pass_on(1, 0)
    pass_on(1, 1)
    pass_on(0, 0)
    relay_on(2)
    second(0)
    relay_on(3)
    pass_on(0, 1)
    need(0)
    need(1)
    lax.fori_loop(0, 2, attend, 0)
    second(1)
    pass_on(1, 2)
    lax.fori_loop(2, 4, attend, 0)
    second(2)
    pass_on(1, 3)
    pass_on(0, 2)
    need(2)
    third(0)
    lax.fori_loop(4, 6, attend, 0)
    pass_on(0, 3)
    need(3)
    third(1)
    lax.fori_loop(6, 8, attend, 0)
    third(2)
    last(0)
    last(1)
    last(2)

    for item in HALO_AFTER_A + HALO_AFTER_B + HALO_AFTER_C:
        halo(*item).wait_send()
    for n in range(4):
        for kv in range(2):
            forward(kv, n).wait_send()

        @pl.when(y_hi == 0)
        def _(n=n):
            relay(n).wait_send()

    for copy in a_copies + c_copies:
        copy.wait_send()
    for side in range(2):
        for c in range(3):
            x1(side, c).wait_send()
            yc(side, c).wait_send()
        for i in range(6):
            x2(side, i).wait_send()
    for d in range(1, 4):

        @pl.when(group + d < 4)
        def _(copy=b_copies[d - 1]):
            copy.wait_send()


def per_device(query1, key1, value1, log_decay, out_weight, query2, key2, value2):
    vm = pltpu.VMEM
    dma = pltpu.SemaphoreType.DMA
    hbm = pl.BlockSpec(memory_space=HBM)
    vmem = pl.BlockSpec(memory_space=vm)
    return pl.pallas_call(
        kernel,
        out_shape=(
            jax.ShapeDtypeStruct((64, PROJ), BF16),
            jax.ShapeDtypeStruct((ROWS, COLS), BF16),
        ),
        in_specs=[hbm, hbm, hbm, vmem, hbm, hbm, hbm, hbm],
        out_specs=(vmem, vmem),
        scratch_shapes=[
            vm((ROWS, COLS), BF16),
            vm((ROWS, COLS), BF16),
            vm((ROWS, COLS), BF16),
            vm((ROWS, COLS), BF16),
            vm((4 * ROWS, COLS), BF16),
            vm((5 * ROWS, COLS), BF16),
            vm((COLS, PROJ), BF16),
            vm((NH, ROWS, 128), F32),
            vm((NH, ROWS), F32),
            vm((ROWS, COLS), F32),
            vm((ROWS, COLS), F32),
            vm((NH, MSG, 128), BF16),
            vm((8, MSG, 128), BF16),
            vm((1, MSG, 128), BF16),
            vm((4, MSG, 128), BF16),
            vm((DH, 128), F32),
            vm((8, DH, 128), BF16),
            vm((8, DH, 128), BF16),
            vm((ROWS, COLS), BF16),
            vm((6, 128, STEP), F32),
            vm((2, 3, 128, STEP), F32),
            vm((2, 3, 128, STEP), BF16),
            vm((2, 3, 128, STEP), BF16),
            vm((2, 6, 128, STEP), BF16),
            vm((2, 6, 128, STEP), BF16),
            vm((2, 3, 64, STEP), BF16),
            vm((2, 3, 64, STEP), BF16),
            vm((2, 256, SPAN), F32),
            vm((2, 256, SPAN), BF16),
            dma((7,)),
            dma((2, 2, 4)),
            dma((4, 2, 4)),
            dma((2, 4)),
            dma((4,)),
            dma((8,)),
            dma((8,)),
            dma((4,)),
            dma((4,)),
            dma((8,)),
            dma((8,)),
            dma((2, 3)),
            dma((2, 3)),
            dma((2, 6)),
            dma((2, 6)),
            dma((2, 3)),
            dma((2, 3)),
        ],
        compiler_params=pltpu.CompilerParams(
            collective_id=0, has_side_effects=True, vmem_limit_bytes=VMEM_LIMIT
        ),
    )(query1, key1, value1, log_decay.T, out_weight, query2, key2, value2)


def solution(mesh):
    spec = P("ctx", "head")
    return jax.shard_map(
        per_device,
        mesh=mesh,
        in_specs=(spec, spec, spec, spec, P("head", None), spec, spec, spec),
        out_specs=(P(("ctx", "head"), None), spec),
        check_vma=False,
    )
```

```python
import math

import jax
import jax.numpy as jnp
from jax import lax
from jax.experimental import pallas as pl
from jax.experimental.pallas import tpu as pltpu
from jax.sharding import PartitionSpec as P

DH = 96
ROWS = 512
COLS = 768
NH = 8
GW = 384
PROJ = 3072
WIN = 256
SPAN = 1792
NEG = -1e30
EPS = 1e-6
MESH = pl.DeviceIdType.MESH
F32 = jnp.float32
BF16 = jnp.bfloat16
HBM = pltpu.MemorySpace.HBM

HALO_AFTER_A = [(0, 1, 0), (1, 0, 0)]
HALO_AFTER_B = [(1, 1, 0)]
HALO_AFTER_C = [(0, 1, 1), (1, 0, 1)]
MSG = 112
STEP = 512


def dot(a, b, ca, cb):
    return lax.dot_general(a, b, (((ca,), (cb,)), ((), ())), preferred_element_type=F32)


def lanes(shape):
    return lax.broadcasted_iota(jnp.int32, shape, len(shape) - 1)


def rows_of(shape):
    return lax.broadcasted_iota(jnp.int32, shape, len(shape) - 2)


def head_window(h):
    start = GW * lax.div(h, 4) + 128 * lax.div(lax.rem(h, 4), 2)
    return pl.multiple_of(start, 128), DH * h - start


def head_mask(low):
    lane = lanes((1, WIN))
    return (lane >= low) & (lane < low + DH)


def same_head(tile):
    row = lax.div(rows_of((GW, 128)), DH)
    col = lax.div(lanes((GW, 128)) + 128 * tile, DH)
    return row == col


def kernel(
    q1h, k1h, v1h, dec, wh, q2h, k2h, v2h,
    lin_out, att_out,
    q1, k1, v1, q2, kk, vv, w,
    crow, ct, cexp, acc, fold, recv_a, tot_b, recv_b, pacc, send_c, recv_c,
    normed, own_part, pass_part, x1s, x1r, x2s, x2r, ys, yr,
    s_scr, p_scr,
    load_sem, halo_send, halo_recv, fwd_send, relay_send, a_send, a_recv, b_send, b_recv, c_send, c_recv,
    x1_send, x1_recv, x2_send, x2_recv, y_send, y_recv,
):
    t, hd = lax.axis_index("ctx"), lax.axis_index("head")
    core, y_hi = lax.rem(t, 2), lax.rem(lax.div(t, 2), 2)
    group, me = lax.div(t, 8), lax.rem(t, 8)
    yl, x = lax.div(hd, 4), lax.rem(hd, 4)
    sibling = t + 1 - 2 * core
    x_to = (yl * 4 + lax.rem(x + 1, 4), yl * 4 + lax.rem(x + 3, 4))
    y_other = (1 - yl) * 4 + x

    related = [
        (lax.rem(t + 2, 32), hd),
        (lax.rem(t + 30, 32), hd),
        (lax.rem(t + 4, 32), hd),
        (lax.rem(t + 28, 32), hd),
        (lax.rem(t + 29 + 6 * core, 32), hd),
        (t, x_to[0]),
        (t, x_to[1]),
        (t, y_other),
    ]
    related += [(8 * group + lax.rem(me + d, 8), hd) for d in range(1, 8)]
    related += [(lax.rem(t + 8 * d, 32), hd) for d in range(1, 4)]
    barrier = pltpu.get_barrier_semaphore()
    for device in related:
        pl.semaphore_signal(barrier, inc=1, device_id=device, device_id_type=MESH)

    own = pl.ds(3 * ROWS, ROWS)
    loads = [
        pltpu.make_async_copy(src, dst, load_sem.at[i])
        for i, (src, dst) in enumerate(
            [(k1h, k1), (v1h, v1), (q1h, q1), (q2h, q2), (k2h, kk.at[own]), (v2h, vv.at[own]), (wh, w)]
        )
    ]
    for copy in loads:
        copy.start()

    def half(g):
        return pl.ds(GW * g, GW)

    def block(slot):
        return pl.ds(pl.multiple_of(slot * ROWS, ROWS), ROWS)

    def halo(kind, kv, g):
        src, dst = ((k2h, kk), (v2h, vv))[kv]
        if kind == 1:
            slot, sem, target = 2 - 2 * core, 2 - 2 * core, lax.rem(t + 1 + 2 * core, 32)
        elif kv == 1:
            slot, sem, target = 1 + 3 * y_hi, 1 + 2 * y_hi, t + 2 - 4 * y_hi
        else:
            slot, sem, target = 1, 1, lax.rem(t + 2, 32)
        return pltpu.make_async_remote_copy(
            src_ref=src.at[:, half(g)],
            dst_ref=dst.at[block(slot), half(g)],
            send_sem=halo_send.at[kind, kv, g],
            recv_sem=halo_recv.at[sem, kv, g],
            device_id=(target, hd),
            device_id_type=MESH,
        )

    def arrived(sem, kv, g):
        dst = (kk, vv)[kv].at[pl.ds((4 if sem == 3 else sem) * ROWS, ROWS), half(g)]
        return pltpu.make_async_remote_copy(
            src_ref=dst,
            dst_ref=dst,
            send_sem=halo_send.at[0, kv, g],
            recv_sem=halo_recv.at[sem, kv, g],
            device_id=(sibling, hd),
            device_id_type=MESH,
        )

    def forward(kv, g):
        buf = (kk, vv)[kv]
        return pltpu.make_async_remote_copy(
            src_ref=buf.at[pl.ds(ROWS, ROWS), half(g)],
            dst_ref=buf.at[block(2 * core), half(g)],
            send_sem=fwd_send.at[kv, g],
            recv_sem=halo_recv.at[2 * core, kv, g],
            device_id=(sibling, hd),
            device_id_type=MESH,
        )

    def relay(g):
        return pltpu.make_async_remote_copy(
            src_ref=vv.at[pl.ds(4 * ROWS, ROWS), half(g)],
            dst_ref=vv.at[pl.ds(ROWS, ROWS), half(g)],
            send_sem=relay_send.at[g],
            recv_sem=halo_recv.at[1, 1, g],
            device_id=(lax.rem(t + 4, 32), hd),
            device_id_type=MESH,
        )

    def relay_on(g):
        @pl.when(y_hi == 0)
        def _():
            arrived(3, 1, g).wait_recv()
            relay(g).start()

    ct[...] = lax.dot_general(
        dec[...],
        (rows_of((ROWS, ROWS)) <= lanes((ROWS, ROWS))).astype(F32),
        (((1,), (0,)), ((), ())),
        precision=lax.Precision.HIGHEST,
        preferred_element_type=F32,
    )
    running = jnp.transpose(jnp.concatenate([ct[...], jnp.zeros((128 - NH, ROWS), F32)], axis=0))
    for h in range(NH):
        crow[h] = jnp.broadcast_to(running[:, h : h + 1], (ROWS, 128))
    lane = lanes((ROWS, 128))
    for g in range(2):
        for tile, cut in enumerate((96, 64, 32)):
            h = 4 * g + tile
            at = pl.ds(GW * g + 128 * tile, 128)
            cexp[:, at] = jnp.where(lane < cut, crow[h], crow[h + 1])

    def message(ref, index, state, decay):
        ref[index, :DH, :] = state.astype(BF16)
        high = decay.astype(BF16)
        rest = decay - high.astype(F32)
        middle = rest.astype(BF16)
        low = (rest - middle.astype(F32)).astype(BF16)
        row = rows_of((MSG - DH, 128))
        parts = [jnp.broadcast_to(p.astype(F32), (MSG - DH, 128)) for p in (high, middle, low)]
        tail = jnp.where(row == 0, parts[0], jnp.where(row == 1, parts[1], jnp.where(row == 2, parts[2], 0.0)))
        ref[index, DH:, :] = tail.astype(BF16)

    def decay_in(ref, index):
        return jnp.sum(ref[index, DH:, :].astype(F32), axis=0, keepdims=True)

    loads[0].wait()
    loads[1].wait()
    for g in range(2):
        c = cexp[:, half(g)]
        kw = (k1[:, half(g)].astype(F32) * jnp.exp(cexp[ROWS - 1 : ROWS, half(g)] - c)).astype(BF16)
        full = dot(kw, v1[:, half(g)], 0, 0)
        total = jnp.zeros((GW, 128), F32)
        for tile in range(3):
            total += jnp.where(same_head(tile), full[:, 128 * tile : 128 * tile + 128], 0.0)
        for i in range(4):
            h = 4 * g + i
            message(fold, h, total[DH * i : DH * i + DH], crow[h, ROWS - 1 : ROWS, :])

    pl.semaphore_wait(barrier, len(related))

    a_copies = []
    for d in range(1, 8):
        to = lax.rem(me + d, 8)
        copy = pltpu.make_async_remote_copy(
            src_ref=fold.at[to], dst_ref=recv_a.at[d], send_sem=a_send.at[d], recv_sem=a_recv.at[d],
            device_id=(8 * group + to, hd), device_id_type=MESH,
        )
        copy.start()
        a_copies.append(copy)
    recv_a[0] = fold[me]
    for item in HALO_AFTER_A:
        halo(*item).start()

    acc[...] = jnp.zeros_like(acc)
    loads[2].wait()
    tri = rows_of((256, 256)) >= lanes((256, 256))

    def intra(h, _):
        start, low = head_window(h)
        window = pl.ds(start, WIN)
        mask = head_mask(low)
        keep = mask.astype(F32).astype(BF16)
        qw = q1[:, window] * keep
        kw = k1[:, window]
        vw = v1[:, window]
        s0 = dot(qw[:256], kw[:256], 1, 1)
        s1 = dot(qw[256:], kw, 1, 1)
        ci = crow[h]
        ci = jnp.concatenate([ci, ci], axis=1)
        cj = ct[pl.ds(h, 1), :]
        e0 = jnp.exp(jnp.where(tri, ci[:256] - cj[:, :256], NEG))
        e10 = jnp.exp(ci[256:] - cj[:, :256])
        e11 = jnp.exp(jnp.where(tri, ci[256:] - cj[:, 256:], NEG))
        m0 = (s0 * e0).astype(BF16)
        m1 = (s1 * jnp.concatenate([e10, e11], axis=1)).astype(BF16)
        acc[pl.ds(0, 256), window] = jnp.where(mask, dot(m0, vw[:256], 1, 0), acc[pl.ds(0, 256), window])
        acc[pl.ds(256, 256), window] = jnp.where(mask, dot(m1, vw, 1, 0), acc[pl.ds(256, 256), window])
        return 0

    lax.fori_loop(0, NH // 2, intra, 0)

    for copy in a_copies:
        copy.wait_recv()

    def member(i):
        return lax.rem(me + 8 - i, 8)

    def then(state, ref, index):
        return jnp.exp(decay_in(ref, index)) * state + ref[index, :DH, :].astype(F32)

    total = jnp.zeros((DH, 128), F32)
    decay = jnp.zeros((1, 128), F32)
    for i in range(8):
        total = then(total, recv_a, member(i))
        decay = decay + decay_in(recv_a, i)
    message(tot_b, 0, total, decay)
    b_copies = []
    for d in range(1, 4):
        copy = pltpu.make_async_remote_copy(
            src_ref=tot_b.at[0], dst_ref=recv_b.at[d], send_sem=b_send.at[d], recv_sem=b_recv.at[d],
            device_id=(lax.rem(t + 8 * d, 32), hd), device_id_type=MESH,
        )
        b_copies.append(copy)

        @pl.when(group + d < 4)
        def _(copy=copy):
            copy.start()

    for item in HALO_AFTER_B:
        halo(*item).start()

    lax.fori_loop(NH // 2, NH, intra, 0)

    pacc[...] = jnp.zeros_like(pacc)
    for d in range(3, 0, -1):

        @pl.when(group >= d)
        def _(d=d):
            b_copies[d - 1].wait_recv()
            pacc[...] = then(pacc[...], recv_b, d)

    state = pacc[...]
    for i in range(8):
        send_c[i] = state.astype(BF16)
        if i < 7:
            state = then(state, recv_a, member(i))
    c_copies = []
    for d in range(1, 8):
        to = lax.rem(me + d, 8)
        copy = pltpu.make_async_remote_copy(
            src_ref=send_c.at[to], dst_ref=recv_c.at[me], send_sem=c_send.at[d], recv_sem=c_recv.at[d],
            device_id=(8 * group + to, hd), device_id_type=MESH,
        )
        copy.start()
        c_copies.append(copy)
    recv_c[me] = send_c[me]
    @pl.when(y_hi == 0)
    def _():
        halo(0, 0, 0).start()

    for item in HALO_AFTER_C:
        halo(*item).start()
    loads[6].wait()
    relay_on(0)
    for copy in c_copies:
        copy.wait_recv()

    for g in range(2):
        states = jnp.concatenate([recv_c[4 * g + i] for i in range(4)], axis=0).astype(F32)
        wide = jnp.concatenate([jnp.where(same_head(i), states, 0.0).astype(BF16) for i in range(3)], axis=1)
        ones = jnp.concatenate([same_head(i).astype(F32).astype(BF16) for i in range(3)], axis=1)
        both = dot(q1[:, half(g)], wide, 1, 0) * jnp.exp(cexp[:, half(g)]) + acc[:, half(g)]
        square = both * both
        high = square.astype(BF16)
        rest = (square - high.astype(F32)).astype(BF16)
        mean = (dot(high, ones, 1, 0) + dot(rest, ones, 1, 0)) * (1.0 / DH)
        normed[:, half(g)] = (both * lax.rsqrt(mean + EPS)).astype(BF16)

    def cols_at(i):
        return pl.ds(pl.multiple_of(STEP * i, STEP), STEP)

    def project(d, i):
        xt = lax.rem(x + d, 4)
        a = jnp.concatenate(
            [
                normed[pl.ds(pl.multiple_of(64 * xt, 64), 64), :],
                normed[pl.ds(pl.multiple_of(256 + 64 * xt, 64), 64), :],
            ],
            axis=0,
        )
        return dot(a, w[:, cols_at(i)], 1, 0)

    def x1(side, c):
        return pltpu.make_async_remote_copy(
            src_ref=x1s.at[side, c], dst_ref=x1r.at[side, c], send_sem=x1_send.at[side, c], recv_sem=x1_recv.at[side, c],
            device_id=(t, x_to[side]), device_id_type=MESH,
        )

    def x2(to, i):
        return pltpu.make_async_remote_copy(
            src_ref=x2s.at[to, i], dst_ref=x2r.at[to, i], send_sem=x2_send.at[to, i], recv_sem=x2_recv.at[to, i],
            device_id=(t, x_to[to]), device_id_type=MESH,
        )

    def yc(side, c):
        return pltpu.make_async_remote_copy(
            src_ref=ys.at[side, c], dst_ref=yr.at[side, c], send_sem=y_send.at[side, c], recv_sem=y_recv.at[side, c],
            device_id=(t, y_other), device_id_type=MESH,
        )

    def first(c, _):
        for side in range(2):
            x1s[side, c] = project(2, c + 3 * side).astype(BF16)
            x1(side, c).start()
        return 0

    def alone(c, _):
        for side in range(2):
            x2s[side, c + 3 - 3 * side] = project(1 + 2 * side, c + 3 - 3 * side).astype(BF16)
        return 0

    def kept(c, _):
        for side in range(2):
            pass_part[side, c] = project(1 + 2 * side, c + 3 * side)
        return 0

    def mine(i, _):
        own_part[i] = project(0, i)
        return 0

    lax.fori_loop(0, 3, first, 0)

    @pl.when(y_hi == 1)
    def _():
        halo(0, 0, 0).start()

    halo(0, 0, 1).start()
    halo(1, 1, 1).start()
    lax.fori_loop(0, 3, alone, 0)
    for side in range(2):
        x2(side, 3 - 3 * side).start()
    lax.fori_loop(0, 3, kept, 0)
    lax.fori_loop(0, 6, mine, 0)

    def second(c):
        for side in range(2):
            x1(side, c).wait_recv()
            x2s[side, c + 3 * side] = (pass_part[side, c] + x1r[side, c].astype(F32)).astype(BF16)
            x2(side, c + 3 * side).start()
        if c < 2:
            for side in range(2):
                x2(side, c + 1 + 3 - 3 * side).start()

    mine_rows = pl.ds(pl.multiple_of(64 * yl, 64), 64)
    their_rows = pl.ds(pl.multiple_of(64 * (1 - yl), 64), 64)

    def third(c):
        for side in range(2):
            i = c + 3 * side
            x2(0, i).wait_recv()
            x2(1, i).wait_recv()

            def total(rows):
                return own_part[i, rows] + x2r[0, i, rows].astype(F32) + x2r[1, i, rows].astype(F32)

            ys[side, c] = total(their_rows).astype(BF16)
            yc(side, c).start()
            own_part[i, mine_rows] = total(mine_rows)

    def last(c):
        for side in range(2):
            i = c + 3 * side
            yc(side, c).wait_recv()
            lin_out[:, pl.ds(STEP * i, STEP)] = (own_part[i, mine_rows] + yr[side, c].astype(F32)).astype(BF16)

    def pass_on(g):
        for kv in range(2):
            arrived(1, kv, g).wait_recv()
            forward(kv, g).start()

    def need(g):
        for kv in range(2):
            for slot in (0, 2):
                arrived(slot, kv, g).wait_recv()

    scale = (1.0 / math.sqrt(DH)) * math.log2(math.e)
    upper = lanes((256, 256)) > rows_of((256, 256))

    def attend(h, _):
        start, low = head_window(h)
        window = pl.ds(start, WIN)
        mask = head_mask(low)
        keep = mask.astype(F32).astype(BF16)
        for i in range(2):
            keys = pl.ds(256 * i, SPAN)
            qw = q2[pl.ds(256 * i, 256), window] * keep
            s_scr[i] = dot(qw, kk[keys, window], 1, 1)
            tops = []
            for n in range(7):
                cols = pl.ds(256 * n, 256)
                if n == 0:
                    s_scr[i, :, cols] = jnp.where(upper, s_scr[i, :, cols], NEG)
                if n == 6:
                    s_scr[i, :, cols] = jnp.where(tri, s_scr[i, :, cols], NEG)
                block = s_scr[i, :, cols]
                top = jnp.maximum(block[:, :128], block[:, 128:])
                first = 3 - (i + n) // 2
                if first > 0:
                    top = jnp.minimum(top, jnp.where(t >= first, 1e38, -1e38))
                tops.append(top)
            while len(tops) > 1:
                tops = [jnp.maximum(*tops[n : n + 2]) if n + 1 < len(tops) else tops[n] for n in range(0, len(tops), 2)]
            peak = jnp.max(tops[0], axis=1, keepdims=True) * scale
            total = jnp.zeros((256, 128), F32)
            for n in range(7):
                cols = pl.ds(256 * n, 256)
                first = 3 - (i + n) // 2
                shift = peak + jnp.where(t >= first, 0.0, 1e30) if first > 0 else peak
                e = jnp.exp2(s_scr[i, :, cols] * scale - shift)
                total += e[:, :128] + e[:, 128:]
                p_scr[i, :, cols] = e.astype(BF16)
            out = dot(p_scr[i], vv[keys, window], 1, 0) * (1.0 / jnp.sum(total, axis=1, keepdims=True))
            rows = pl.ds(256 * i, 256)
            old = att_out[rows, window].astype(F32)
            att_out[rows, window] = jnp.where(mask, out, old).astype(BF16)
        return 0

    att_out[...] = jnp.zeros_like(att_out)
    for i in (3, 4, 5):
        loads[i].wait()
    second(0)
    pass_on(0)
    second(1)
    relay_on(1)
    second(2)
    need(0)
    lax.fori_loop(0, 3, attend, 0)
    third(0)
    lax.fori_loop(3, 4, attend, 0)
    pass_on(1)
    need(1)
    third(1)
    lax.fori_loop(4, 6, attend, 0)
    third(2)
    lax.fori_loop(6, 8, attend, 0)
    last(0)
    last(1)
    last(2)

    for item in HALO_AFTER_A + HALO_AFTER_B + HALO_AFTER_C + [(0, 0, 0), (0, 0, 1), (1, 1, 1)]:
        halo(*item).wait_send()
    for g in range(2):
        for kv in range(2):
            forward(kv, g).wait_send()

        @pl.when(y_hi == 0)
        def _(g=g):
            relay(g).wait_send()

    for copy in a_copies + c_copies:
        copy.wait_send()
    for side in range(2):
        for c in range(3):
            x1(side, c).wait_send()
            yc(side, c).wait_send()
        for i in range(6):
            x2(side, i).wait_send()
    for d in range(1, 4):

        @pl.when(group + d < 4)
        def _(copy=b_copies[d - 1]):
            copy.wait_send()


def per_device(query1, key1, value1, log_decay, out_weight, query2, key2, value2):
    vm = pltpu.VMEM
    dma = pltpu.SemaphoreType.DMA
    hbm = pl.BlockSpec(memory_space=HBM)
    vmem = pl.BlockSpec(memory_space=vm)
    return pl.pallas_call(
        kernel,
        out_shape=(
            jax.ShapeDtypeStruct((64, PROJ), BF16),
            jax.ShapeDtypeStruct((ROWS, COLS), BF16),
        ),
        in_specs=[hbm, hbm, hbm, vmem, hbm, hbm, hbm, hbm],
        out_specs=(vmem, vmem),
        scratch_shapes=[
            vm((ROWS, COLS), BF16),
            vm((ROWS, COLS), BF16),
            vm((ROWS, COLS), BF16),
            vm((ROWS, COLS), BF16),
            vm((4 * ROWS, COLS), BF16),
            vm((5 * ROWS, COLS), BF16),
            vm((COLS, PROJ), BF16),
            vm((NH, ROWS, 128), F32),
            vm((NH, ROWS), F32),
            vm((ROWS, COLS), F32),
            vm((ROWS, COLS), F32),
            vm((NH, MSG, 128), BF16),
            vm((8, MSG, 128), BF16),
            vm((1, MSG, 128), BF16),
            vm((4, MSG, 128), BF16),
            vm((DH, 128), F32),
            vm((8, DH, 128), BF16),
            vm((8, DH, 128), BF16),
            vm((ROWS, COLS), BF16),
            vm((6, 128, STEP), F32),
            vm((2, 3, 128, STEP), F32),
            vm((2, 3, 128, STEP), BF16),
            vm((2, 3, 128, STEP), BF16),
            vm((2, 6, 128, STEP), BF16),
            vm((2, 6, 128, STEP), BF16),
            vm((2, 3, 64, STEP), BF16),
            vm((2, 3, 64, STEP), BF16),
            vm((2, 256, SPAN), F32),
            vm((2, 256, SPAN), BF16),
            dma((7,)),
            dma((2, 2, 2)),
            dma((4, 2, 2)),
            dma((2, 2)),
            dma((2,)),
            dma((8,)),
            dma((8,)),
            dma((4,)),
            dma((4,)),
            dma((8,)),
            dma((8,)),
            dma((2, 3)),
            dma((2, 3)),
            dma((2, 6)),
            dma((2, 6)),
            dma((2, 3)),
            dma((2, 3)),
        ],
        compiler_params=pltpu.CompilerParams(
            collective_id=0, has_side_effects=True, vmem_limit_bytes=53 * 1024 * 1024
        ),
    )(query1, key1, value1, log_decay.T, out_weight, query2, key2, value2)


def solution(mesh):
    spec = P("ctx", "head")
    return jax.shard_map(
        per_device,
        mesh=mesh,
        in_specs=(spec, spec, spec, spec, P("head", None), spec, spec, spec),
        out_specs=(P(("ctx", "head"), None), spec),
        check_vma=False,
    )
```

```python
import math

import jax
import jax.numpy as jnp
from jax import lax
from jax.experimental import pallas as pl
from jax.experimental.pallas import tpu as pltpu
from jax.sharding import PartitionSpec as P

DH = 96
ROWS = 512
COLS = 768
NH = 8
GW = 384
PROJ = 3072
WIN = 256
SPAN = 1792
NEG = -1e30
EPS = 1e-6
MESH = pl.DeviceIdType.MESH
F32 = jnp.float32
BF16 = jnp.bfloat16
HBM = pltpu.MemorySpace.HBM

HALO_AFTER_A = [(0, 1, 0), (1, 0, 0)]
HALO_AFTER_B = [(1, 1, 0)]
HALO_AFTER_C = [(0, 1, 1), (1, 0, 1)]
MSG = 112
STEP = 512


def dot(a, b, ca, cb):
    return lax.dot_general(a, b, (((ca,), (cb,)), ((), ())), preferred_element_type=F32)


def lanes(shape):
    return lax.broadcasted_iota(jnp.int32, shape, len(shape) - 1)


def rows_of(shape):
    return lax.broadcasted_iota(jnp.int32, shape, len(shape) - 2)


def head_window(h):
    start = GW * lax.div(h, 4) + 128 * lax.div(lax.rem(h, 4), 2)
    return pl.multiple_of(start, 128), DH * h - start


def head_mask(low):
    lane = lanes((1, WIN))
    return (lane >= low) & (lane < low + DH)


def same_head(tile):
    row = lax.div(rows_of((GW, 128)), DH)
    col = lax.div(lanes((GW, 128)) + 128 * tile, DH)
    return row == col


def kernel(
    q1h, k1h, v1h, dec, wh, q2h, k2h, v2h,
    lin_out, att_out,
    q1, k1, v1, q2, kk, vv, w,
    crow, ct, cexp, acc, fold, recv_a, tot_b, recv_b, pacc, send_c, recv_c,
    normed, own_part, pass_part, x1s, x1r, x2s, x2r, ys, yr,
    s_scr, p_scr,
    load_sem, halo_send, halo_recv, fwd_send, relay_send, a_send, a_recv, b_send, b_recv, c_send, c_recv,
    x1_send, x1_recv, x2_send, x2_recv, y_send, y_recv,
):
    t, hd = lax.axis_index("ctx"), lax.axis_index("head")
    core, y_hi = lax.rem(t, 2), lax.rem(lax.div(t, 2), 2)
    group, me = lax.div(t, 8), lax.rem(t, 8)
    yl, x = lax.div(hd, 4), lax.rem(hd, 4)
    sibling = t + 1 - 2 * core
    x_to = (yl * 4 + lax.rem(x + 1, 4), yl * 4 + lax.rem(x + 3, 4))
    y_other = (1 - yl) * 4 + x

    related = [
        (lax.rem(t + 2, 32), hd),
        (lax.rem(t + 30, 32), hd),
        (lax.rem(t + 4, 32), hd),
        (lax.rem(t + 28, 32), hd),
        (lax.rem(t + 29 + 6 * core, 32), hd),
        (t, x_to[0]),
        (t, x_to[1]),
        (t, y_other),
    ]
    related += [(8 * group + lax.rem(me + d, 8), hd) for d in range(1, 8)]
    related += [(lax.rem(t + 8 * d, 32), hd) for d in range(1, 4)]
    barrier = pltpu.get_barrier_semaphore()
    for device in related:
        pl.semaphore_signal(barrier, inc=1, device_id=device, device_id_type=MESH)

    own = pl.ds(3 * ROWS, ROWS)
    loads = [
        pltpu.make_async_copy(src, dst, load_sem.at[i])
        for i, (src, dst) in enumerate(
            [(k1h, k1), (v1h, v1), (q1h, q1), (q2h, q2), (k2h, kk.at[own]), (v2h, vv.at[own]), (wh, w)]
        )
    ]
    for copy in loads:
        copy.start()

    def half(g):
        return pl.ds(GW * g, GW)

    def block(slot):
        return pl.ds(pl.multiple_of(slot * ROWS, ROWS), ROWS)

    def piece(slot, kv, n):
        rows = 256 if kv == 1 and n > 0 else ROWS
        start = slot * ROWS + (256 if n == 2 else 0)
        return pl.ds(pl.multiple_of(start, 256), rows), half(min(n, 1))

    def halo(kind, kv, n):
        src, dst = ((k2h, kk), (v2h, vv))[kv]
        if kind == 1:
            slot, sem, target = 2 - 2 * core, 2 - 2 * core, lax.rem(t + 1 + 2 * core, 32)
        elif kv == 1 and n < 2:
            slot, sem, target = 1 + 3 * y_hi, 1 + 2 * y_hi, t + 2 - 4 * y_hi
        else:
            slot, sem, target = 1, 1, lax.rem(t + 2, 32)
        return pltpu.make_async_remote_copy(
            src_ref=src.at[piece(0, kv, n)],
            dst_ref=dst.at[piece(slot, kv, n)],
            send_sem=halo_send.at[kind, kv, n],
            recv_sem=halo_recv.at[sem, kv, n],
            device_id=(target, hd),
            device_id_type=MESH,
        )

    def arrived(sem, kv, n):
        dst = (kk, vv)[kv].at[piece(4 if sem == 3 else sem, kv, n)]
        return pltpu.make_async_remote_copy(
            src_ref=dst,
            dst_ref=dst,
            send_sem=halo_send.at[0, kv, n],
            recv_sem=halo_recv.at[sem, kv, n],
            device_id=(sibling, hd),
            device_id_type=MESH,
        )

    def forward(kv, n):
        buf = (kk, vv)[kv]
        return pltpu.make_async_remote_copy(
            src_ref=buf.at[piece(1, kv, n)],
            dst_ref=buf.at[piece(2 * core, kv, n)],
            send_sem=fwd_send.at[kv, n],
            recv_sem=halo_recv.at[2 * core, kv, n],
            device_id=(sibling, hd),
            device_id_type=MESH,
        )

    def relay(n):
        return pltpu.make_async_remote_copy(
            src_ref=vv.at[piece(4, 1, n)],
            dst_ref=vv.at[piece(1, 1, n)],
            send_sem=relay_send.at[n],
            recv_sem=halo_recv.at[1, 1, n],
            device_id=(lax.rem(t + 4, 32), hd),
            device_id_type=MESH,
        )

    def relay_on(n):
        @pl.when(y_hi == 0)
        def _():
            arrived(3, 1, n).wait_recv()
            relay(n).start()

    ct[...] = lax.dot_general(
        dec[...],
        (rows_of((ROWS, ROWS)) <= lanes((ROWS, ROWS))).astype(F32),
        (((1,), (0,)), ((), ())),
        precision=lax.Precision.HIGHEST,
        preferred_element_type=F32,
    )
    running = jnp.transpose(jnp.concatenate([ct[...], jnp.zeros((128 - NH, ROWS), F32)], axis=0))
    for h in range(NH):
        crow[h] = jnp.broadcast_to(running[:, h : h + 1], (ROWS, 128))
    lane = lanes((ROWS, 128))
    for g in range(2):
        for tile, cut in enumerate((96, 64, 32)):
            h = 4 * g + tile
            at = pl.ds(GW * g + 128 * tile, 128)
            cexp[:, at] = jnp.where(lane < cut, crow[h], crow[h + 1])

    def message(ref, index, state, decay):
        ref[index, :DH, :] = state.astype(BF16)
        high = decay.astype(BF16)
        rest = decay - high.astype(F32)
        middle = rest.astype(BF16)
        low = (rest - middle.astype(F32)).astype(BF16)
        row = rows_of((MSG - DH, 128))
        parts = [jnp.broadcast_to(p.astype(F32), (MSG - DH, 128)) for p in (high, middle, low)]
        tail = jnp.where(row == 0, parts[0], jnp.where(row == 1, parts[1], jnp.where(row == 2, parts[2], 0.0)))
        ref[index, DH:, :] = tail.astype(BF16)

    def decay_in(ref, index):
        return jnp.sum(ref[index, DH:, :].astype(F32), axis=0, keepdims=True)

    loads[0].wait()
    loads[1].wait()
    for g in range(2):
        c = cexp[:, half(g)]
        kw = (k1[:, half(g)].astype(F32) * jnp.exp(cexp[ROWS - 1 : ROWS, half(g)] - c)).astype(BF16)
        full = dot(kw, v1[:, half(g)], 0, 0)
        total = jnp.zeros((GW, 128), F32)
        for tile in range(3):
            total += jnp.where(same_head(tile), full[:, 128 * tile : 128 * tile + 128], 0.0)
        for i in range(4):
            h = 4 * g + i
            message(fold, h, total[DH * i : DH * i + DH], crow[h, ROWS - 1 : ROWS, :])

    pl.semaphore_wait(barrier, len(related))

    a_copies = []
    for d in range(1, 8):
        to = lax.rem(me + d, 8)
        copy = pltpu.make_async_remote_copy(
            src_ref=fold.at[to], dst_ref=recv_a.at[d], send_sem=a_send.at[d], recv_sem=a_recv.at[d],
            device_id=(8 * group + to, hd), device_id_type=MESH,
        )
        copy.start()
        a_copies.append(copy)
    recv_a[0] = fold[me]
    for item in HALO_AFTER_A:
        halo(*item).start()

    acc[...] = jnp.zeros_like(acc)
    loads[2].wait()
    tri = rows_of((256, 256)) >= lanes((256, 256))

    def intra(h, _):
        start, low = head_window(h)
        window = pl.ds(start, WIN)
        mask = head_mask(low)
        keep = mask.astype(F32).astype(BF16)
        qw = q1[:, window] * keep
        kw = k1[:, window]
        vw = v1[:, window]
        s0 = dot(qw[:256], kw[:256], 1, 1)
        s1 = dot(qw[256:], kw, 1, 1)
        ci = crow[h]
        ci = jnp.concatenate([ci, ci], axis=1)
        cj = ct[pl.ds(h, 1), :]
        e0 = jnp.exp(jnp.where(tri, ci[:256] - cj[:, :256], NEG))
        e10 = jnp.exp(ci[256:] - cj[:, :256])
        e11 = jnp.exp(jnp.where(tri, ci[256:] - cj[:, 256:], NEG))
        m0 = (s0 * e0).astype(BF16)
        m1 = (s1 * jnp.concatenate([e10, e11], axis=1)).astype(BF16)
        acc[pl.ds(0, 256), window] = jnp.where(mask, dot(m0, vw[:256], 1, 0), acc[pl.ds(0, 256), window])
        acc[pl.ds(256, 256), window] = jnp.where(mask, dot(m1, vw, 1, 0), acc[pl.ds(256, 256), window])
        return 0

    lax.fori_loop(0, NH // 2, intra, 0)

    for copy in a_copies:
        copy.wait_recv()

    def member(i):
        return lax.rem(me + 8 - i, 8)

    def then(state, ref, index):
        return jnp.exp(decay_in(ref, index)) * state + ref[index, :DH, :].astype(F32)

    total = jnp.zeros((DH, 128), F32)
    decay = jnp.zeros((1, 128), F32)
    for i in range(8):
        total = then(total, recv_a, member(i))
        decay = decay + decay_in(recv_a, i)
    message(tot_b, 0, total, decay)
    b_copies = []
    for d in range(1, 4):
        copy = pltpu.make_async_remote_copy(
            src_ref=tot_b.at[0], dst_ref=recv_b.at[d], send_sem=b_send.at[d], recv_sem=b_recv.at[d],
            device_id=(lax.rem(t + 8 * d, 32), hd), device_id_type=MESH,
        )
        b_copies.append(copy)

        @pl.when(group + d < 4)
        def _(copy=copy):
            copy.start()

    for item in HALO_AFTER_B:
        halo(*item).start()

    lax.fori_loop(NH // 2, NH, intra, 0)

    pacc[...] = jnp.zeros_like(pacc)
    for d in range(3, 0, -1):

        @pl.when(group >= d)
        def _(d=d):
            b_copies[d - 1].wait_recv()
            pacc[...] = then(pacc[...], recv_b, d)

    state = pacc[...]
    for i in range(8):
        send_c[i] = state.astype(BF16)
        if i < 7:
            state = then(state, recv_a, member(i))
    c_copies = []
    for d in range(1, 8):
        to = lax.rem(me + d, 8)
        copy = pltpu.make_async_remote_copy(
            src_ref=send_c.at[to], dst_ref=recv_c.at[me], send_sem=c_send.at[d], recv_sem=c_recv.at[d],
            device_id=(8 * group + to, hd), device_id_type=MESH,
        )
        copy.start()
        c_copies.append(copy)
    recv_c[me] = send_c[me]
    @pl.when(y_hi == 0)
    def _():
        halo(0, 0, 0).start()

    for item in HALO_AFTER_C:
        halo(*item).start()
    loads[6].wait()
    relay_on(0)
    for copy in c_copies:
        copy.wait_recv()

    for g in range(2):
        states = jnp.concatenate([recv_c[4 * g + i] for i in range(4)], axis=0).astype(F32)
        wide = jnp.concatenate([jnp.where(same_head(i), states, 0.0).astype(BF16) for i in range(3)], axis=1)
        ones = jnp.concatenate([same_head(i).astype(F32).astype(BF16) for i in range(3)], axis=1)
        both = dot(q1[:, half(g)], wide, 1, 0) * jnp.exp(cexp[:, half(g)]) + acc[:, half(g)]
        square = both * both
        high = square.astype(BF16)
        rest = (square - high.astype(F32)).astype(BF16)
        mean = (dot(high, ones, 1, 0) + dot(rest, ones, 1, 0)) * (1.0 / DH)
        normed[:, half(g)] = (both * lax.rsqrt(mean + EPS)).astype(BF16)

    def cols_at(i):
        return pl.ds(pl.multiple_of(STEP * i, STEP), STEP)

    def project(d, i):
        xt = lax.rem(x + d, 4)
        a = jnp.concatenate(
            [
                normed[pl.ds(pl.multiple_of(64 * xt, 64), 64), :],
                normed[pl.ds(pl.multiple_of(256 + 64 * xt, 64), 64), :],
            ],
            axis=0,
        )
        return dot(a, w[:, cols_at(i)], 1, 0)

    def x1(side, c):
        return pltpu.make_async_remote_copy(
            src_ref=x1s.at[side, c], dst_ref=x1r.at[side, c], send_sem=x1_send.at[side, c], recv_sem=x1_recv.at[side, c],
            device_id=(t, x_to[side]), device_id_type=MESH,
        )

    def x2(to, i):
        return pltpu.make_async_remote_copy(
            src_ref=x2s.at[to, i], dst_ref=x2r.at[to, i], send_sem=x2_send.at[to, i], recv_sem=x2_recv.at[to, i],
            device_id=(t, x_to[to]), device_id_type=MESH,
        )

    def yc(side, c):
        return pltpu.make_async_remote_copy(
            src_ref=ys.at[side, c], dst_ref=yr.at[side, c], send_sem=y_send.at[side, c], recv_sem=y_recv.at[side, c],
            device_id=(t, y_other), device_id_type=MESH,
        )

    def first(c, _):
        for side in range(2):
            x1s[side, c] = project(2, c + 3 * side).astype(BF16)
            x1(side, c).start()
        return 0

    def alone(c, _):
        for side in range(2):
            x2s[side, c + 3 - 3 * side] = project(1 + 2 * side, c + 3 - 3 * side).astype(BF16)
        return 0

    def kept(c, _):
        for side in range(2):
            pass_part[side, c] = project(1 + 2 * side, c + 3 * side)
        return 0

    def mine(i, _):
        own_part[i] = project(0, i)
        return 0

    lax.fori_loop(0, 3, first, 0)

    @pl.when(y_hi == 1)
    def _():
        halo(0, 0, 0).start()

    halo(0, 1, 2).start()
    halo(1, 1, 1).start()
    halo(0, 0, 1).start()
    halo(1, 1, 2).start()
    lax.fori_loop(0, 3, alone, 0)
    for side in range(2):
        x2(side, 3 - 3 * side).start()
    lax.fori_loop(0, 3, kept, 0)
    lax.fori_loop(0, 6, mine, 0)

    def second(c):
        for side in range(2):
            x1(side, c).wait_recv()
            x2s[side, c + 3 * side] = (pass_part[side, c] + x1r[side, c].astype(F32)).astype(BF16)
            x2(side, c + 3 * side).start()
        if c < 2:
            for side in range(2):
                x2(side, c + 1 + 3 - 3 * side).start()

    mine_rows = pl.ds(pl.multiple_of(64 * yl, 64), 64)
    their_rows = pl.ds(pl.multiple_of(64 * (1 - yl), 64), 64)

    def third(c):
        for side in range(2):
            i = c + 3 * side
            x2(0, i).wait_recv()
            x2(1, i).wait_recv()

            def total(rows):
                return own_part[i, rows] + x2r[0, i, rows].astype(F32) + x2r[1, i, rows].astype(F32)

            ys[side, c] = total(their_rows).astype(BF16)
            yc(side, c).start()
            own_part[i, mine_rows] = total(mine_rows)

    def last(c):
        for side in range(2):
            i = c + 3 * side
            yc(side, c).wait_recv()
            lin_out[:, pl.ds(STEP * i, STEP)] = (own_part[i, mine_rows] + yr[side, c].astype(F32)).astype(BF16)

    def pass_on(g):
        for kv, n in ((1, 0), (0, 0)) if g == 0 else ((1, 1), (1, 2), (0, 1)):
            arrived(1, kv, n).wait_recv()
            forward(kv, n).start()

    def need(g):
        for kv, n in ((1, 0), (0, 0)) if g == 0 else ((1, 1), (1, 2), (0, 1)):
            for slot in (0, 2):
                arrived(slot, kv, n).wait_recv()

    scale = (1.0 / math.sqrt(DH)) * math.log2(math.e)
    upper = lanes((256, 256)) > rows_of((256, 256))

    def attend(h, _):
        start, low = head_window(h)
        window = pl.ds(start, WIN)
        mask = head_mask(low)
        keep = mask.astype(F32).astype(BF16)
        for i in range(2):
            keys = pl.ds(256 * i, SPAN)
            qw = q2[pl.ds(256 * i, 256), window] * keep
            s_scr[i] = dot(qw, kk[keys, window], 1, 1)
            tops = []
            for n in range(7):
                cols = pl.ds(256 * n, 256)
                if n == 0:
                    s_scr[i, :, cols] = jnp.where(upper, s_scr[i, :, cols], NEG)
                if n == 6:
                    s_scr[i, :, cols] = jnp.where(tri, s_scr[i, :, cols], NEG)
                block = s_scr[i, :, cols]
                top = jnp.maximum(block[:, :128], block[:, 128:])
                first = 3 - (i + n) // 2
                if first > 0:
                    top = jnp.minimum(top, jnp.where(t >= first, 1e38, -1e38))
                tops.append(top)
            while len(tops) > 1:
                tops = [jnp.maximum(*tops[n : n + 2]) if n + 1 < len(tops) else tops[n] for n in range(0, len(tops), 2)]
            peak = jnp.max(tops[0], axis=1, keepdims=True) * scale
            total = jnp.zeros((256, 128), F32)
            for n in range(7):
                cols = pl.ds(256 * n, 256)
                first = 3 - (i + n) // 2
                shift = peak + jnp.where(t >= first, 0.0, 1e30) if first > 0 else peak
                e = jnp.exp2(s_scr[i, :, cols] * scale - shift)
                total += e[:, :128] + e[:, 128:]
                p_scr[i, :, cols] = e.astype(BF16)
            out = dot(p_scr[i], vv[keys, window], 1, 0) * (1.0 / jnp.sum(total, axis=1, keepdims=True))
            rows = pl.ds(256 * i, 256)
            old = att_out[rows, window].astype(F32)
            att_out[rows, window] = jnp.where(mask, out, old).astype(BF16)
        return 0

    att_out[...] = jnp.zeros_like(att_out)
    for i in (3, 4, 5):
        loads[i].wait()
    second(0)
    pass_on(0)
    second(1)
    relay_on(1)
    second(2)
    need(0)
    lax.fori_loop(0, 3, attend, 0)
    third(0)
    lax.fori_loop(3, 4, attend, 0)
    pass_on(1)
    need(1)
    third(1)
    lax.fori_loop(4, 6, attend, 0)
    third(2)
    lax.fori_loop(6, 8, attend, 0)
    last(0)
    last(1)
    last(2)

    for item in HALO_AFTER_A + HALO_AFTER_B + HALO_AFTER_C + [(0, 0, 0), (0, 1, 2), (1, 1, 1), (0, 0, 1), (1, 1, 2)]:
        halo(*item).wait_send()
    for kv, n in ((0, 0), (0, 1), (1, 0), (1, 1), (1, 2)):
        forward(kv, n).wait_send()
    for n in range(2):

        @pl.when(y_hi == 0)
        def _(n=n):
            relay(n).wait_send()

    for copy in a_copies + c_copies:
        copy.wait_send()
    for side in range(2):
        for c in range(3):
            x1(side, c).wait_send()
            yc(side, c).wait_send()
        for i in range(6):
            x2(side, i).wait_send()
    for d in range(1, 4):

        @pl.when(group + d < 4)
        def _(copy=b_copies[d - 1]):
            copy.wait_send()


def per_device(query1, key1, value1, log_decay, out_weight, query2, key2, value2):
    vm = pltpu.VMEM
    dma = pltpu.SemaphoreType.DMA
    hbm = pl.BlockSpec(memory_space=HBM)
    vmem = pl.BlockSpec(memory_space=vm)
    return pl.pallas_call(
        kernel,
        out_shape=(
            jax.ShapeDtypeStruct((64, PROJ), BF16),
            jax.ShapeDtypeStruct((ROWS, COLS), BF16),
        ),
        in_specs=[hbm, hbm, hbm, vmem, hbm, hbm, hbm, hbm],
        out_specs=(vmem, vmem),
        scratch_shapes=[
            vm((ROWS, COLS), BF16),
            vm((ROWS, COLS), BF16),
            vm((ROWS, COLS), BF16),
            vm((ROWS, COLS), BF16),
            vm((4 * ROWS, COLS), BF16),
            vm((5 * ROWS, COLS), BF16),
            vm((COLS, PROJ), BF16),
            vm((NH, ROWS, 128), F32),
            vm((NH, ROWS), F32),
            vm((ROWS, COLS), F32),
            vm((ROWS, COLS), F32),
            vm((NH, MSG, 128), BF16),
            vm((8, MSG, 128), BF16),
            vm((1, MSG, 128), BF16),
            vm((4, MSG, 128), BF16),
            vm((DH, 128), F32),
            vm((8, DH, 128), BF16),
            vm((8, DH, 128), BF16),
            vm((ROWS, COLS), BF16),
            vm((6, 128, STEP), F32),
            vm((2, 3, 128, STEP), F32),
            vm((2, 3, 128, STEP), BF16),
            vm((2, 3, 128, STEP), BF16),
            vm((2, 6, 128, STEP), BF16),
            vm((2, 6, 128, STEP), BF16),
            vm((2, 3, 64, STEP), BF16),
            vm((2, 3, 64, STEP), BF16),
            vm((2, 256, SPAN), F32),
            vm((2, 256, SPAN), BF16),
            dma((7,)),
            dma((2, 2, 3)),
            dma((4, 2, 3)),
            dma((2, 3)),
            dma((2,)),
            dma((8,)),
            dma((8,)),
            dma((4,)),
            dma((4,)),
            dma((8,)),
            dma((8,)),
            dma((2, 3)),
            dma((2, 3)),
            dma((2, 6)),
            dma((2, 6)),
            dma((2, 3)),
            dma((2, 3)),
        ],
        compiler_params=pltpu.CompilerParams(
            collective_id=0, has_side_effects=True, vmem_limit_bytes=53 * 1024 * 1024
        ),
    )(query1, key1, value1, log_decay.T, out_weight, query2, key2, value2)


def solution(mesh):
    spec = P("ctx", "head")
    return jax.shard_map(
        per_device,
        mesh=mesh,
        in_specs=(spec, spec, spec, spec, P("head", None), spec, spec, spec),
        out_specs=(P(("ctx", "head"), None), spec),
        check_vma=False,
    )
```
